128 devices in a mesh: ctx: 16 (over y_lo, z, core), head: 8 (over y_hi, x).
Axes of the slice: x: 4, y: 4 (y_hi: 2, y_lo: 2; y = y_hi * 2 + y_lo), z: 4, core: 2. Of those that a mesh axis runs over, the one named last changes fastest.
Arguments:
- queries: bfloat16 [16384, 4096], P('ctx', 'head'), may hold values from -8 to 8
- keys: bfloat16 [16384, 1024], P('ctx', 'head'), may hold values from -8 to 8
Outputs:
- grad_queries: float32 [16384, 4096], P('ctx', 'head')
- grad_blocks: float32 [32, 1024], P('ctx', 'head')
- loss: float32 [], replicated
The draws below stay inside these ranges and needn't reach their ends.
All inputs are finite; a program needn't handle non-finite values.
Results may differ from the reference program's by a relative error of at most 0.00045.
Values may be sent and summed in bfloat16 or wider, within the bound.
A program may use at most 64 MiB of HBM per device.

```python
import jax
import jax.numpy as jnp
from jax import lax

D_HEAD = 128
HEADS = 32
KV_HEADS = 8
BLOCK = 512
SEQ = 16384


def draw_keys(key, part):
    key_noise = jnp.clip(jax.random.normal(jax.random.fold_in(key, 1), (SEQ, KV_HEADS * D_HEAD), jnp.float32), -3.0, 3.0)
    block_part = jnp.clip(jax.random.normal(jax.random.fold_in(key, 2), (SEQ // BLOCK, KV_HEADS * D_HEAD), jnp.float32), -3.5, 3.5)
    return (key_noise + jnp.repeat(block_part, BLOCK, axis=0)).astype(jnp.bfloat16)


def draw_queries(key, part):
    row_width = HEADS * D_HEAD
    return jnp.clip(jax.random.normal(jax.random.fold_in(key, 4), (SEQ, row_width), jnp.float32), -4.0, 4.0).astype(jnp.bfloat16)


def setup_inputs(seed: int = 0) -> dict:
    key_list = jax.random.split(jax.random.key(seed), 3)
    return {
        "queries": draw_queries(jax.random.fold_in(key_list[2], 71), 0),
        "keys": draw_keys(jax.random.fold_in(key_list[2], 71), 0),
    }


def head_pass(query_head, key_head, pooled_head):
    group_size = query_head.shape[1]
    score_scale = D_HEAD ** -0.5
    block_total = SEQ // BLOCK

    def per_block(totals, block_index):
        grad_pool, entropy_sum = totals
        row_start = (block_index * BLOCK).astype(jnp.int32)
        query_rows = lax.dynamic_slice_in_dim(query_head, row_start, BLOCK, 0).astype(jnp.float32)
        query_pos = row_start + jnp.arange(BLOCK, dtype=jnp.int32)

        def key_step(key_index, running):
            row_peak, block_mass = running
            key_start = (key_index * BLOCK).astype(jnp.int32)
            key_rows = lax.dynamic_slice_in_dim(key_head, key_start, BLOCK, 0).astype(jnp.float32)
            scores = jnp.einsum("qrd,kd->qrk", query_rows, key_rows) * score_scale
            key_pos = key_start + jnp.arange(BLOCK, dtype=jnp.int32)
            causal_mask = key_pos[None, None, :] <= query_pos[:, None, None]
            new_peak = jnp.maximum(row_peak, jnp.max(jnp.where(causal_mask, scores, -1e30), axis=-1))
            probability = jnp.where(causal_mask, jnp.exp(scores - new_peak[..., None]), 0.0)
            block_mass = block_mass * jnp.exp(row_peak - new_peak)[..., None]
            block_mass = lax.dynamic_update_slice_in_dim(block_mass, jnp.sum(probability, axis=-1)[..., None], key_index, 2)
            return new_peak, block_mass

        initial = (jnp.full((BLOCK, group_size), -1e30, jnp.float32), jnp.zeros((BLOCK, group_size, block_total), jnp.float32))
        row_peak, block_mass = lax.fori_loop(0, block_index + 1, key_step, initial)
        teacher = block_mass / jnp.sum(block_mass, axis=-1, keepdims=True)
        gate_logits = jnp.einsum("qrd,bd->qrb", query_rows, pooled_head, precision=lax.Precision.HIGHEST)
        allowed = (jnp.arange(block_total, dtype=jnp.int32) <= block_index)[None, None, :]
        logit_peak = jnp.max(jnp.where(allowed, gate_logits, -1e30), axis=-1, keepdims=True)
        weights = jnp.where(allowed, jnp.exp(gate_logits - logit_peak), 0.0)
        weight_sum = jnp.sum(weights, axis=-1, keepdims=True)
        student = weights / weight_sum
        cross_entropy = logit_peak[..., 0] + jnp.log(weight_sum[..., 0]) - jnp.sum(teacher * gate_logits, axis=-1)
        gate_error = student - teacher
        grad_query = jnp.einsum("qrb,bd->qrd", gate_error, pooled_head, precision=lax.Precision.HIGHEST)
        grad_pool = grad_pool + jnp.einsum("qrb,qrd->bd", gate_error, query_rows, precision=lax.Precision.HIGHEST)
        return (grad_pool, entropy_sum + jnp.sum(cross_entropy)), grad_query

    initial = (jnp.zeros((block_total, D_HEAD), jnp.float32), jnp.zeros((), jnp.float32))
    (grad_pool, entropy_sum), grad_query = lax.scan(per_block, initial, jnp.arange(block_total, dtype=jnp.int32))
    return grad_query.reshape(SEQ, group_size, D_HEAD), grad_pool, entropy_sum


def one_head(operands):
    return head_pass(operands[0], operands[1], operands[2])


def reference(queries, keys):
    group_size = HEADS // KV_HEADS
    query_heads = queries.reshape(SEQ, KV_HEADS, group_size, D_HEAD).transpose(1, 0, 2, 3)
    key_heads = keys.reshape(SEQ, KV_HEADS, D_HEAD).transpose(1, 0, 2)
    pooled = jnp.sum(keys.astype(jnp.float32).reshape(SEQ // BLOCK, BLOCK, KV_HEADS, D_HEAD), axis=1) / BLOCK
    pooled_heads = pooled.transpose(1, 0, 2)
    grad_query, grad_pool, entropy_sum = lax.map(one_head, (query_heads, key_heads, pooled_heads))
    grad_queries = grad_query.transpose(1, 0, 2, 3).reshape(SEQ, HEADS * D_HEAD)
    grad_blocks = (grad_pool / BLOCK).transpose(1, 0, 2).reshape(SEQ // BLOCK, KV_HEADS * D_HEAD)
    loss = jnp.sum(entropy_sum) / (SEQ * HEADS)
    return grad_queries, grad_blocks, loss
```

```python
import functools
import math

import jax
import jax.numpy as jnp
from jax import lax
from jax.experimental import pallas as pl
from jax.experimental.pallas import tpu as pltpu
from jax.sharding import PartitionSpec as P

D_HEAD = 128
HEADS = 32
KV_HEADS = 8
BLOCK = 512
GROUP = HEADS // KV_HEADS
NEG_FLOOR = -1e30
SCALE = D_HEAD ** (-0.5)
EXP2_SCALE = SCALE * math.log2(math.e)
TOTAL_LOW = 1e-25
TOTAL_HIGH = 3e38
MESH = pl.DeviceIdType.MESH
NT = (((1,), (1,)), ((), ()))
NN = (((1,), (0,)), ((), ()))
TN = (((0,), (0,)), ((), ()))
F32 = jnp.float32
BF16 = jnp.bfloat16


def split3(x):
    a = x.astype(BF16)
    rest = x - a.astype(F32)
    b = rest.astype(BF16)
    c = (rest - b.astype(F32)).astype(BF16)
    return a, b, c


def kernel(
    safe,
    n_ctx,
    n_head,
    q_hbm,
    k_hbm,
    gq_ref,
    gb_ref,
    st_ref,
    q_ref,
    kbuf,
    mass,
    peak,
    pool,
    parts,
    gbs,
    gbr,
    hsend,
    hrecv,
    loc_sem,
    own_send,
    fwd_send,
    key_recv,
    r1_send,
    r1_recv,
    r2_send,
    r2_recv,
):
    rank = lax.axis_index("ctx")
    head = lax.axis_index("head")
    chip = rank // 2
    core = rank % 2
    sibling = chip * 2 + 1 - core
    rows = q_ref.shape[0]
    n_chip = n_ctx // 2
    n_block = mass.shape[1]

    barrier = pltpu.get_barrier_semaphore()

    @pl.loop(1, n_ctx)
    def _(o):
        pl.semaphore_signal(
            barrier, inc=1, device_id={"ctx": lax.rem(rank + o, n_ctx)}, device_id_type=MESH
        )

    @pl.loop(1, n_head)
    def _(o):
        pl.semaphore_signal(
            barrier, inc=1, device_id={"head": lax.rem(head + o, n_head)}, device_id_type=MESH
        )

    q_copy = pltpu.make_async_copy(q_hbm, q_ref, loc_sem.at[0])
    q_copy.start()
    k_copy = pltpu.make_async_copy(k_hbm, kbuf.at[rank], loc_sem.at[1])
    k_copy.start()
    mass[...] = jnp.zeros_like(mass)
    pool[...] = jnp.zeros_like(pool)
    if safe:
        peak[...] = jnp.full_like(peak, NEG_FLOOR)
    k_copy.wait()
    pl.semaphore_wait(barrier, n_ctx + n_head - 2)

    def own_copy(to_chip):
        return pltpu.make_async_remote_copy(
            src_ref=kbuf.at[rank],
            dst_ref=kbuf.at[rank],
            send_sem=own_send.at[to_chip],
            recv_sem=key_recv.at[rank],
            device_id={"ctx": to_chip * 2 + core},
            device_id_type=MESH,
        )

    def sibling_copy(piece, sem):
        return pltpu.make_async_remote_copy(
            src_ref=kbuf.at[piece],
            dst_ref=kbuf.at[piece],
            send_sem=sem,
            recv_sem=key_recv.at[piece],
            device_id={"ctx": sibling},
            device_id_type=MESH,
        )

    @pl.when(core == 0)
    def _():
        sibling_copy(rank, own_send.at[chip]).start()

    @pl.loop(chip + 1, n_chip)
    def _(c):
        own_copy(c).start()

    q_copy.wait()

    def tile_sum(h, keys, row_low, row_count, mask):
        q = q_ref[pl.ds(row_low, row_count), pl.ds(pl.multiple_of(h * D_HEAD, D_HEAD), D_HEAD)]
        s = lax.dot_general(keys, q, NT, preferred_element_type=F32)
        if safe:
            shown = s if mask is None else jnp.where(mask, s, NEG_FLOOR)
            top = jnp.max(shown, axis=0, keepdims=True)
            s = s - top
        else:
            top = None
        p = jnp.exp2(s * EXP2_SCALE)
        if mask is not None:
            p = jnp.where(mask, p, 0.0)
        return jnp.sum(p, axis=0, keepdims=True), top

    def put(h, block, low, count, value):
        mass[h, pl.ds(block, 1), pl.ds(low, count)] = value[0]
        if safe:
            peak[h, pl.ds(block, 1), pl.ds(low, count)] = value[1]

    def pool_of(keys):
        return jnp.sum(keys.astype(F32), axis=0, keepdims=True) * (1.0 / BLOCK)

    own_block = rank * 2
    tri = lax.broadcasted_iota(jnp.int32, (BLOCK, BLOCK), 0) <= lax.broadcasted_iota(
        jnp.int32, (BLOCK, BLOCK), 1
    )

    def diagonal(h, _):
        first = kbuf[rank, :BLOCK]
        second = kbuf[rank, BLOCK:]
        put(h, own_block, 0, BLOCK, tile_sum(h, first, 0, BLOCK, tri))
        put(h, own_block, BLOCK, BLOCK, tile_sum(h, first, BLOCK, BLOCK, None))
        put(h, own_block + 1, BLOCK, BLOCK, tile_sum(h, second, BLOCK, BLOCK, tri))
        return 0

    pool[pl.ds(own_block, 1), :] = pool_of(kbuf[rank, :BLOCK])
    pool[pl.ds(own_block + 1, 1), :] = pool_of(kbuf[rank, BLOCK:])
    lax.fori_loop(0, GROUP, diagonal, 0)

    def piece_step(i, _):
        later = i - core
        back = 1 + later // 2
        phase = later % 2
        far = (chip - back) * 2 + jnp.where(phase == 0, core, 1 - core)
        piece = jnp.where(later < 0, rank - 1, far)
        sibling_copy(piece, own_send.at[chip]).wait_recv()

        @pl.when((later >= 0) & (phase == 0))
        def _():
            sibling_copy(piece, fwd_send.at[chip - back]).start()

        for half in range(2):
            keys = kbuf[piece, half * BLOCK : (half + 1) * BLOCK]
            pool[pl.ds(piece * 2 + half, 1), :] = pool_of(keys)
            for h in range(GROUP):
                put(h, piece * 2 + half, 0, rows, tile_sum(h, keys, 0, rows, None))
        return 0

    lax.fori_loop(0, rank, piece_step, 0)

    p1, p2, p3 = split3(pool[...])
    pool_rows = jnp.concatenate([p1, p2, p3], axis=0)
    pool_stack = jnp.concatenate([p1, p2, p3, p1, p2, p1], axis=0)
    block_id = lax.broadcasted_iota(jnp.int32, (n_block, rows), 0)
    row_block = own_block + lax.broadcasted_iota(jnp.int32, (n_block, rows), 1) // BLOCK
    allowed = block_id <= row_block
    grad_sum = jnp.zeros((n_block, D_HEAD), F32)
    entropy = jnp.zeros((1, rows), F32)
    bad = jnp.zeros((1, rows), F32)
    for h in range(GROUP):
        q = q_ref[:, h * D_HEAD : (h + 1) * D_HEAD]
        g3 = lax.dot_general(pool_rows, q, NT, preferred_element_type=F32)
        logits = (g3[2 * n_block :] + g3[n_block : 2 * n_block]) + g3[:n_block]
        m = mass[h]
        if safe:
            top = jnp.max(peak[h], axis=0, keepdims=True)
            m = m * jnp.exp2((peak[h] - top) * EXP2_SCALE)
        total = jnp.sum(m, axis=0, keepdims=True)
        fine = (total > TOTAL_LOW) & (total < TOTAL_HIGH)
        bad = bad + jnp.where(fine, 0.0, 1.0)
        teacher = m / total
        top = jnp.max(jnp.where(allowed, logits, NEG_FLOOR), axis=0, keepdims=True)
        weights = jnp.where(allowed, jnp.exp(logits - top), 0.0)
        weight_sum = jnp.sum(weights, axis=0, keepdims=True)
        student = weights / weight_sum
        entropy = entropy + (
            top + jnp.log(weight_sum) - jnp.sum(teacher * logits, axis=0, keepdims=True)
        )
        e1, e2, e3 = split3(student - teacher)
        three = jnp.concatenate([e1, e2, e3], axis=0)
        parts[h] = three
        g = lax.dot_general(three, q, NN, preferred_element_type=F32)
        grad_sum = grad_sum + ((g[2 * n_block :] + g[n_block : 2 * n_block]) + g[:n_block])

    grad_sum = grad_sum * (1.0 / BLOCK)
    lane_sum = lambda x: sum(x[:, i * 128 : (i + 1) * 128] for i in range(rows // 128))
    entropy_lanes = lane_sum(entropy)
    bad_lanes = lane_sum(bad)
    for t in range(n_ctx):
        gbs[t, 0:2, :] = grad_sum[2 * t : 2 * t + 2, :]
        gbs[t, 2:3, :] = entropy_lanes
        gbs[t, 3:4, :] = bad_lanes
        gbs[t, 4:8, :] = jnp.zeros((4, 128), F32)

    def r1_copy(slot, to):
        return pltpu.make_async_remote_copy(
            src_ref=gbs.at[to],
            dst_ref=gbr.at[slot],
            send_sem=r1_send.at[to],
            recv_sem=r1_recv.at[slot],
            device_id={"ctx": to},
            device_id_type=MESH,
        )

    @pl.loop(1, n_ctx)
    def _(o):
        r1_copy(rank, lax.rem(rank + o, n_ctx)).start()

    gbr[rank] = gbs[rank]

    def grad_rows(h):
        e1 = parts[h, :n_block]
        e2 = parts[h, n_block : 2 * n_block]
        e3 = parts[h, 2 * n_block :]
        stack = jnp.concatenate([e1, e1, e1, e2, e2, e3], axis=0)
        gq_ref[:, h * D_HEAD : (h + 1) * D_HEAD] = lax.dot_general(
            stack, pool_stack, TN, preferred_element_type=F32
        )

    for h in range(GROUP):
        grad_rows(h)

    @pl.loop(1, n_ctx)
    def _(o):
        other = lax.rem(rank + o, n_ctx)
        r1_copy(other, other).wait_recv()

    whole = gbr[0]
    for t in range(1, n_ctx):
        whole = whole + gbr[t]
    gb_ref[...] = whole[0:2]
    hsend[...] = whole

    def r2_copy(slot, to):
        return pltpu.make_async_remote_copy(
            src_ref=hsend,
            dst_ref=hrecv.at[slot],
            send_sem=r2_send.at[to],
            recv_sem=r2_recv.at[slot],
            device_id={"head": to},
            device_id_type=MESH,
        )

    @pl.loop(1, n_head)
    def _(o):
        r2_copy(head, lax.rem(head + o, n_head)).start()

    hrecv[head] = whole

    @pl.loop(1, n_ctx)
    def _(o):
        other = lax.rem(rank + o, n_ctx)
        r1_copy(rank, other).wait_send()

    @pl.when(core == 0)
    def _():
        sibling_copy(rank, own_send.at[chip]).wait_send()

    @pl.loop(chip + 1, n_chip)
    def _(c):
        own_copy(c).wait_send()

    @pl.loop(0, chip)
    def _(c):
        sibling_copy(rank, fwd_send.at[c]).wait_send()

    @pl.loop(1, n_head)
    def _(o):
        other = lax.rem(head + o, n_head)
        r2_copy(other, other).wait_recv()

    final = hrecv[0]
    for t in range(1, n_head):
        final = final + hrecv[t]
    st_ref[...] = jnp.broadcast_to(
        jnp.sum(final, axis=1, keepdims=True) * (1.0 / (rows * n_ctx * HEADS)), (8, 128)
    )

    @pl.loop(1, n_head)
    def _(o):
        other = lax.rem(head + o, n_head)
        r2_copy(head, other).wait_send()


def run(safe, n_ctx, n_head, queries, keys):
    rows = queries.shape[0]
    n_block = n_ctx * rows // BLOCK
    n_chip = n_ctx // 2
    dma = pltpu.SemaphoreType.DMA
    return pl.pallas_call(
        functools.partial(kernel, safe, n_ctx, n_head),
        out_shape=(
            jax.ShapeDtypeStruct((rows, GROUP * D_HEAD), F32),
            jax.ShapeDtypeStruct((rows // BLOCK, D_HEAD), F32),
            jax.ShapeDtypeStruct((8, 128), F32),
        ),
        in_specs=[pl.BlockSpec(memory_space=pl.ANY)] * 2,
        out_specs=(pl.BlockSpec(memory_space=pltpu.VMEM),) * 3,
        scratch_shapes=[
            pltpu.VMEM((rows, GROUP * D_HEAD), BF16),
            pltpu.VMEM((n_ctx, rows, D_HEAD), BF16),
            pltpu.VMEM((GROUP, n_block, rows), F32),
            pltpu.VMEM((GROUP, n_block, rows) if safe else (8, 128), F32),
            pltpu.VMEM((n_block, D_HEAD), F32),
            pltpu.VMEM((GROUP, 3 * n_block, rows), BF16),
            pltpu.VMEM((n_ctx, 8, 128), F32),
            pltpu.VMEM((n_ctx, 8, 128), F32),
            pltpu.VMEM((8, 128), F32),
            pltpu.VMEM((n_head, 8, 128), F32),
            dma((2,)),
            dma((n_chip,)),
            dma((n_chip,)),
            dma((n_ctx,)),
            dma((n_ctx,)),
            dma((n_ctx,)),
            dma((n_head,)),
            dma((n_head,)),
        ],
        compiler_params=pltpu.CompilerParams(
            collective_id=1 if safe else 0,
            has_side_effects=True,
            vmem_limit_bytes=48 * 1024 * 1024,
        ),
        name="gate_safe" if safe else "gate_fast",
    )(queries, keys)


def solution(mesh):
    n_ctx, n_head = mesh.shape["ctx"], mesh.shape["head"]

    def local(queries, keys):
        fast = run(False, n_ctx, n_head, queries, keys)
        ok = fast[2][3, 0] == 0.0
        out = lax.cond(
            ok,
            lambda: fast,
            lambda: run(True, n_ctx, n_head, queries, keys),
        )
        return out[0], out[1], out[2][2, 0]

    return jax.shard_map(
        local,
        mesh=mesh,
        in_specs=(P("ctx", "head"), P("ctx", "head")),
        out_specs=(P("ctx", "head"), P("ctx", "head"), P()),
        check_vma=False,
    )
```

```python
import functools
import math

import jax
import jax.numpy as jnp
from jax import lax
from jax.experimental import pallas as pl
from jax.experimental.pallas import tpu as pltpu
from jax.sharding import PartitionSpec as P

D_HEAD = 128
HEADS = 32
KV_HEADS = 8
BLOCK = 512
GROUP = HEADS // KV_HEADS
NEG_FLOOR = -1e30
SCALE = D_HEAD ** (-0.5)
EXP2_SCALE = SCALE * math.log2(math.e)
TOTAL_LOW = 1e-25
TOTAL_HIGH = 3e38
MESH = pl.DeviceIdType.MESH
NT = (((1,), (1,)), ((), ()))
NN = (((1,), (0,)), ((), ()))
TN = (((0,), (0,)), ((), ()))
F32 = jnp.float32
BF16 = jnp.bfloat16


def split3(x):
    a = x.astype(BF16)
    rest = x - a.astype(F32)
    b = rest.astype(BF16)
    c = (rest - b.astype(F32)).astype(BF16)
    return a, b, c


def kernel(
    safe,
    n_ctx,
    n_head,
    q_hbm,
    k_hbm,
    gq_ref,
    gb_ref,
    st_ref,
    q_ref,
    kbuf,
    mass,
    peak,
    pool,
    parts,
    ship_out,
    ship_in,
    gbs,
    gbr,
    hsend,
    hrecv,
    loc_sem,
    q_sem,
    own_send,
    fwd_send,
    up_send,
    key_recv,
    ship_send,
    ship_recv,
    r1_send,
    r1_recv,
    r2_send,
    r2_recv,
):
    rank = lax.axis_index("ctx")
    head = lax.axis_index("head")
    half_ctx = n_ctx // 2
    n_z = half_ctx // 2
    upper = rank // half_ctx
    zee = lax.rem(rank, half_ctx) // 2
    core = lax.rem(rank, 2)
    plane = upper * half_ctx
    sibling = plane + zee * 2 + 1 - core
    partner = lax.rem(rank + half_ctx, n_ctx)
    rows = mass.shape[2]
    n_block = mass.shape[1]
    width = GROUP * D_HEAD
    kept = width // 2

    barrier = pltpu.get_barrier_semaphore()

    @pl.loop(1, n_ctx)
    def _(o):
        pl.semaphore_signal(
            barrier, inc=1, device_id={"ctx": lax.rem(rank + o, n_ctx)}, device_id_type=MESH
        )

    @pl.loop(1, n_head)
    def _(o):
        pl.semaphore_signal(
            barrier, inc=1, device_id={"head": lax.rem(head + o, n_head)}, device_id_type=MESH
        )

    q_copy = pltpu.make_async_copy(q_hbm, q_ref.at[:, :width], loc_sem.at[0])
    q_copy.start()
    k_copy = pltpu.make_async_copy(k_hbm, kbuf.at[rank], loc_sem.at[1])
    k_copy.start()
    mass[...] = jnp.zeros_like(mass)
    pool[...] = jnp.zeros_like(pool)
    if safe:
        peak[...] = jnp.full_like(peak, NEG_FLOOR)
    k_copy.wait()
    pl.semaphore_wait(barrier, n_ctx + n_head - 2)

    def key_copy(piece, to, sem):
        return pltpu.make_async_remote_copy(
            src_ref=kbuf.at[piece],
            dst_ref=kbuf.at[piece],
            send_sem=sem,
            recv_sem=key_recv.at[piece],
            device_id={"ctx": to},
            device_id_type=MESH,
        )

    def own_across(o):
        return key_copy(rank, plane + lax.rem(zee + o, n_z) * 2 + core, own_send.at[o])

    own_sibling = key_copy(rank, sibling, own_send.at[0])
    own_up = key_copy(rank, partner, own_send.at[n_z])
    q_ship = pltpu.make_async_remote_copy(
        src_ref=q_hbm.at[:, kept:],
        dst_ref=q_ref.at[:, width:],
        send_sem=q_sem.at[0],
        recv_sem=q_sem.at[1],
        device_id={"ctx": partner},
        device_id_type=MESH,
    )

    @pl.when(upper == 0)
    def _():
        own_sibling.start()
        own_up.start()
        for o in (n_z - 1, *range(1, n_z - 1)):
            own_across(o).start()

    @pl.when(upper == 1)
    def _():
        q_ship.start()

        @pl.when(core == 0)
        def _():
            own_sibling.start()

        @pl.loop(1, n_z - zee)
        def _(o):
            own_across(o).start()

    q_copy.wait()

    def tile_sum(h, keys, row_low, row_count, mask):
        q = q_ref[pl.ds(row_low, row_count), pl.ds(pl.multiple_of(h * D_HEAD, D_HEAD), D_HEAD)]
        s = lax.dot_general(keys, q, NT, preferred_element_type=F32)
        if safe:
            shown = s if mask is None else jnp.where(mask, s, NEG_FLOOR)
            top = jnp.max(shown, axis=0, keepdims=True)
            s = s - top
        else:
            top = None
        p = jnp.exp2(s * EXP2_SCALE)
        if mask is not None:
            p = jnp.where(mask, p, 0.0)
        return jnp.sum(p, axis=0, keepdims=True), top

    def put(h, block, low, count, value):
        mass[h, pl.ds(block, 1), pl.ds(low, count)] = value[0]
        if safe:
            peak[h, pl.ds(block, 1), pl.ds(low, count)] = value[1]

    def pool_of(keys):
        return jnp.sum(keys.astype(F32), axis=0, keepdims=True) * (1.0 / BLOCK)

    own_block = rank * 2
    tri = lax.broadcasted_iota(jnp.int32, (BLOCK, BLOCK), 0) <= lax.broadcasted_iota(
        jnp.int32, (BLOCK, BLOCK), 1
    )

    def diagonal(h, _):
        first = kbuf[rank, :BLOCK]
        second = kbuf[rank, BLOCK:]
        put(h, own_block, 0, BLOCK, tile_sum(h, first, 0, BLOCK, tri))
        put(h, own_block, BLOCK, BLOCK, tile_sum(h, first, BLOCK, BLOCK, None))
        put(h, own_block + 1, BLOCK, BLOCK, tile_sum(h, second, BLOCK, BLOCK, tri))
        return 0

    pool[pl.ds(own_block, 1), :] = pool_of(kbuf[rank, :BLOCK])
    pool[pl.ds(own_block + 1, 1), :] = pool_of(kbuf[rank, BLOCK:])
    lax.fori_loop(0, GROUP, diagonal, 0)

    def ship_copy(piece):
        return pltpu.make_async_remote_copy(
            src_ref=ship_out.at[piece],
            dst_ref=ship_in.at[piece],
            send_sem=ship_send.at[piece],
            recv_sem=ship_recv.at[piece],
            device_id={"ctx": partner},
            device_id_type=MESH,
        )

    def arrival_z(o):
        return lax.rem(zee + jnp.where(o == 1, n_z - 1, jnp.where(o == 0, 0, o - 1)), n_z)

    n_low = half_ctx - 1 + half_ctx
    n_up = core + 2 * zee + half_ctx
    n_steps = jnp.where(upper == 0, n_low, n_up)

    def step(i, _):
        lo_phase = lax.rem(i + 1, 2)
        lo_core = jnp.where(lo_phase == 0, core, 1 - core)
        lo_piece = arrival_z((i + 1) // 2) * 2 + lo_core
        lo_ship = i >= half_ctx - 1
        lo_piece = jnp.where(lo_ship, i - (half_ctx - 1), lo_piece)
        lo_direct = (lo_phase == 0) & (i < half_ctx - 1)
        j = jnp.maximum(i - core, 0)
        up_phase = lax.rem(j, 2)
        up_core = jnp.where(up_phase == 0, core, 1 - core)
        up_own = j < 2 * zee
        up_z = jnp.where(up_own, zee - 1 - j // 2, arrival_z((j - 2 * zee) // 2))
        up_piece = jnp.where(up_own, half_ctx, 0) + up_z * 2 + up_core
        up_sib = i < core
        up_piece = jnp.where(up_sib, rank - 1, up_piece)
        up_direct = (up_phase == 0) & jnp.logical_not(up_sib)
        low = upper == 0
        piece = jnp.where(low, lo_piece, up_piece)
        direct = jnp.where(low, lo_direct.astype(jnp.int32), up_direct.astype(jnp.int32)) == 1
        shipped = low & lo_ship
        full = jnp.where(low, jnp.where(lo_piece < rank, 2, 0), jnp.where(up_own | up_sib, 2, 1))
        hp_low = jnp.where(shipped, 2, 0)
        hp_high = jnp.where(shipped, 3, full)

        @pl.when(jnp.logical_not(shipped))
        def _():
            key_copy(piece, sibling, own_send.at[0]).wait_recv()

        @pl.when(direct)
        def _():
            key_copy(piece, sibling, fwd_send.at[piece]).start()

        @pl.when(direct & low)
        def _():
            key_copy(piece, partner, up_send.at[piece]).start()

        @pl.when(low & (i == half_ctx - 1))
        def _():
            q_ship.wait_recv()

        def unit(hp, _):
            for half in range(2):
                keys = kbuf[piece, half * BLOCK : (half + 1) * BLOCK]
                block = piece * 2 + half
                pool[pl.ds(block, 1), :] = pool_of(keys)
                for j in range(2):
                    h = hp * 2 + j
                    put(h, block, 0, rows, tile_sum(h, keys, 0, rows, None))
            return 0

        lax.fori_loop(hp_low, hp_high, unit, 0)

        @pl.when(shipped)
        def _():
            for k, source in enumerate((mass, peak) if safe else (mass,)):
                for j in range(2):
                    for half in range(2):
                        for part in range(2):
                            ship_out[piece, k * 8 + j * 4 + half * 2 + part, :] = source[
                                GROUP + j, piece * 2 + half, part * BLOCK : (part + 1) * BLOCK
                            ]
            ship_copy(piece).start()

        return 0

    lax.fori_loop(0, n_steps, step, 0)

    def collect():
        def one(piece, _):
            ship_copy(piece).wait_recv()
            for k, target in enumerate((mass, peak) if safe else (mass,)):
                for j in range(2):
                    for half in range(2):
                        for part in range(2):
                            target[
                                2 + j, piece * 2 + half, part * BLOCK : (part + 1) * BLOCK
                            ] = ship_in[piece, k * 8 + j * 4 + half * 2 + part, :]
            return 0

        lax.fori_loop(0, half_ctx, one, 0)

    p1, p2, p3 = split3(pool[...])
    pool_rows = jnp.concatenate([p1, p2, p3], axis=0)
    pool_stack = jnp.concatenate([p1, p2, p3, p1, p2, p1], axis=0)
    block_id = lax.broadcasted_iota(jnp.int32, (n_block, rows), 0)
    row_block = own_block + lax.broadcasted_iota(jnp.int32, (n_block, rows), 1) // BLOCK
    allowed = block_id <= row_block
    grad_sum = jnp.zeros((n_block, D_HEAD), F32)
    entropy = jnp.zeros((1, rows), F32)
    bad = jnp.zeros((1, rows), F32)
    for h in range(GROUP):
        if h == 2:
            pl.when(upper == 1)(collect)
        q = q_ref[:, h * D_HEAD : (h + 1) * D_HEAD]
        g3 = lax.dot_general(pool_rows, q, NT, preferred_element_type=F32)
        logits = (g3[2 * n_block :] + g3[n_block : 2 * n_block]) + g3[:n_block]
        m = mass[h]
        if safe:
            top = jnp.max(peak[h], axis=0, keepdims=True)
            m = m * jnp.exp2((peak[h] - top) * EXP2_SCALE)
        total = jnp.sum(m, axis=0, keepdims=True)
        fine = (total > TOTAL_LOW) & (total < TOTAL_HIGH)
        bad = bad + jnp.where(fine, 0.0, 1.0)
        teacher = m / total
        top = jnp.max(jnp.where(allowed, logits, NEG_FLOOR), axis=0, keepdims=True)
        weights = jnp.where(allowed, jnp.exp(logits - top), 0.0)
        weight_sum = jnp.sum(weights, axis=0, keepdims=True)
        student = weights / weight_sum
        entropy = entropy + (
            top + jnp.log(weight_sum) - jnp.sum(teacher * logits, axis=0, keepdims=True)
        )
        e1, e2, e3 = split3(student - teacher)
        three = jnp.concatenate([e1, e2, e3], axis=0)
        parts[h] = three
        g = lax.dot_general(three, q, NN, preferred_element_type=F32)
        grad_sum = grad_sum + ((g[2 * n_block :] + g[n_block : 2 * n_block]) + g[:n_block])

    grad_sum = grad_sum * (1.0 / BLOCK)
    lane_sum = lambda x: sum(x[:, i * 128 : (i + 1) * 128] for i in range(rows // 128))
    entropy_lanes = lane_sum(entropy)
    bad_lanes = lane_sum(bad)
    for t in range(n_ctx):
        gbs[t, 0:2, :] = grad_sum[2 * t : 2 * t + 2, :]
        gbs[t, 2:3, :] = entropy_lanes
        gbs[t, 3:4, :] = bad_lanes
        gbs[t, 4:8, :] = jnp.zeros((4, 128), F32)

    def r1_copy(slot, to):
        return pltpu.make_async_remote_copy(
            src_ref=gbs.at[to],
            dst_ref=gbr.at[slot],
            send_sem=r1_send.at[to],
            recv_sem=r1_recv.at[slot],
            device_id={"ctx": to},
            device_id_type=MESH,
        )

    @pl.loop(1, n_ctx)
    def _(o):
        r1_copy(rank, lax.rem(rank + o, n_ctx)).start()

    gbr[rank] = gbs[rank]

    def grad_rows(h):
        e1 = parts[h, :n_block]
        e2 = parts[h, n_block : 2 * n_block]
        e3 = parts[h, 2 * n_block :]
        stack = jnp.concatenate([e1, e1, e1, e2, e2, e3], axis=0)
        gq_ref[:, h * D_HEAD : (h + 1) * D_HEAD] = lax.dot_general(
            stack, pool_stack, TN, preferred_element_type=F32
        )

    for h in range(GROUP):
        grad_rows(h)

    @pl.loop(1, n_ctx)
    def _(o):
        other = lax.rem(rank + o, n_ctx)
        r1_copy(other, other).wait_recv()

    whole = gbr[0]
    for t in range(1, n_ctx):
        whole = whole + gbr[t]
    gb_ref[...] = whole[0:2]
    hsend[...] = whole

    def r2_copy(slot, to):
        return pltpu.make_async_remote_copy(
            src_ref=hsend,
            dst_ref=hrecv.at[slot],
            send_sem=r2_send.at[to],
            recv_sem=r2_recv.at[slot],
            device_id={"head": to},
            device_id_type=MESH,
        )

    @pl.loop(1, n_head)
    def _(o):
        r2_copy(head, lax.rem(head + o, n_head)).start()

    hrecv[head] = whole

    @pl.loop(1, n_ctx)
    def _(o):
        other = lax.rem(rank + o, n_ctx)
        r1_copy(rank, other).wait_send()

    @pl.when(upper == 0)
    def _():
        own_sibling.wait_send()
        own_up.wait_send()
        for o in range(1, n_z):
            own_across(o).wait_send()
            piece = lax.rem(zee + o, n_z) * 2 + core
            key_copy(piece, sibling, fwd_send.at[piece]).wait_send()
            key_copy(piece, partner, up_send.at[piece]).wait_send()
        for piece in range(half_ctx):
            ship_copy(piece).wait_send()

    @pl.when(upper == 1)
    def _():
        q_ship.wait_send()

        @pl.when(core == 0)
        def _():
            own_sibling.wait_send()

        @pl.loop(1, n_z - zee)
        def _(o):
            own_across(o).wait_send()

        @pl.loop(0, zee)
        def _(z):
            piece = half_ctx + z * 2 + core
            key_copy(piece, sibling, fwd_send.at[piece]).wait_send()

        for z in range(n_z):
            piece = z * 2 + core
            key_copy(piece, sibling, fwd_send.at[piece]).wait_send()

    @pl.loop(1, n_head)
    def _(o):
        other = lax.rem(head + o, n_head)
        r2_copy(other, other).wait_recv()

    final = hrecv[0]
    for t in range(1, n_head):
        final = final + hrecv[t]
    st_ref[...] = jnp.broadcast_to(
        jnp.sum(final, axis=1, keepdims=True) * (1.0 / (rows * n_ctx * HEADS)), (8, 128)
    )

    @pl.loop(1, n_head)
    def _(o):
        other = lax.rem(head + o, n_head)
        r2_copy(head, other).wait_send()


def run(safe, n_ctx, n_head, queries, keys):
    rows = queries.shape[0]
    n_block = n_ctx * rows // BLOCK
    half_ctx = n_ctx // 2
    ship_rows = 16 if safe else 8
    dma = pltpu.SemaphoreType.DMA
    return pl.pallas_call(
        functools.partial(kernel, safe, n_ctx, n_head),
        out_shape=(
            jax.ShapeDtypeStruct((rows, GROUP * D_HEAD), F32),
            jax.ShapeDtypeStruct((rows // BLOCK, D_HEAD), F32),
            jax.ShapeDtypeStruct((8, 128), F32),
        ),
        in_specs=[pl.BlockSpec(memory_space=pl.ANY)] * 2,
        out_specs=(pl.BlockSpec(memory_space=pltpu.VMEM),) * 3,
        scratch_shapes=[
            pltpu.VMEM((rows, (GROUP + 2) * D_HEAD), BF16),
            pltpu.VMEM((n_ctx, rows, D_HEAD), BF16),
            pltpu.VMEM((GROUP + 2, n_block, rows), F32),
            pltpu.VMEM((GROUP + 2, n_block, rows) if safe else (8, 128), F32),
            pltpu.VMEM((n_block, D_HEAD), F32),
            pltpu.VMEM((GROUP, 3 * n_block, rows), BF16),
            pltpu.VMEM((half_ctx, ship_rows, BLOCK), F32),
            pltpu.VMEM((half_ctx, ship_rows, BLOCK), F32),
            pltpu.VMEM((n_ctx, 8, 128), F32),
            pltpu.VMEM((n_ctx, 8, 128), F32),
            pltpu.VMEM((8, 128), F32),
            pltpu.VMEM((n_head, 8, 128), F32),
            dma((2,)),
            dma((2,)),
            dma((half_ctx // 2 + 1,)),
            dma((n_ctx,)),
            dma((half_ctx,)),
            dma((n_ctx,)),
            dma((half_ctx,)),
            dma((half_ctx,)),
            dma((n_ctx,)),
            dma((n_ctx,)),
            dma((n_head,)),
            dma((n_head,)),
        ],
        compiler_params=pltpu.CompilerParams(
            collective_id=1 if safe else 0,
            has_side_effects=True,
            vmem_limit_bytes=48 * 1024 * 1024,
        ),
        name="gate_safe" if safe else "gate_fast",
    )(queries, keys)


def solution(mesh):
    n_ctx, n_head = mesh.shape["ctx"], mesh.shape["head"]

    def local(queries, keys):
        fast = run(False, n_ctx, n_head, queries, keys)
        ok = fast[2][3, 0] == 0.0
        out = lax.cond(
            ok,
            lambda: fast,
            lambda: run(True, n_ctx, n_head, queries, keys),
        )
        return out[0], out[1], out[2][2, 0]

    return jax.shard_map(
        local,
        mesh=mesh,
        in_specs=(P("ctx", "head"), P("ctx", "head")),
        out_specs=(P("ctx", "head"), P("ctx", "head"), P()),
        check_vma=False,
    )
```

```python
import functools
import math

import jax
import jax.numpy as jnp
from jax import lax
from jax.experimental import pallas as pl
from jax.experimental.pallas import tpu as pltpu
from jax.sharding import PartitionSpec as P

D_HEAD = 128
HEADS = 32
KV_HEADS = 8
BLOCK = 512
GROUP = HEADS // KV_HEADS
NEG_FLOOR = -1e30
SCALE = D_HEAD ** (-0.5)
EXP2_SCALE = SCALE * math.log2(math.e)
TOTAL_LOW = 1e-25
TOTAL_HIGH = 3e38
MESH = pl.DeviceIdType.MESH
NT = (((1,), (1,)), ((), ()))
NN = (((1,), (0,)), ((), ()))
TN = (((0,), (0,)), ((), ()))
F32 = jnp.float32
BF16 = jnp.bfloat16


def split3(x):
    a = x.astype(BF16)
    rest = x - a.astype(F32)
    b = rest.astype(BF16)
    c = (rest - b.astype(F32)).astype(BF16)
    return a, b, c


def kernel(
    safe,
    n_ctx,
    n_head,
    q_hbm,
    k_hbm,
    gq_ref,
    gb_ref,
    loss_ref,
    bad_ref,
    q_ref,
    kbuf,
    mass,
    peak,
    pool,
    parts,
    ship_out,
    ship_in,
    gbs,
    gbr,
    hsend,
    hrecv,
    loc_sem,
    q_sem,
    own_send,
    fwd_send,
    next_send,
    prev_send,
    key_recv,
    ship_send,
    ship_recv,
    r1_send,
    r1_recv,
    r2_send,
    r2_recv,
):
    rank = lax.axis_index("ctx")
    head = lax.axis_index("head")
    half_ctx = n_ctx // 2
    n_z = half_ctx // 2
    upper = rank // half_ctx
    zee = lax.rem(rank, half_ctx) // 2
    core = lax.rem(rank, 2)
    plane = upper * half_ctx
    sibling = plane + zee * 2 + 1 - core
    partner = lax.rem(rank + half_ctx, n_ctx)
    rows = mass.shape[2]
    n_block = mass.shape[1]
    width = GROUP * D_HEAD
    kept = width // 2

    barrier = pltpu.get_barrier_semaphore()

    @pl.loop(1, n_ctx)
    def _(o):
        pl.semaphore_signal(
            barrier, inc=1, device_id={"ctx": lax.rem(rank + o, n_ctx)}, device_id_type=MESH
        )

    @pl.loop(1, n_head)
    def _(o):
        pl.semaphore_signal(
            barrier, inc=1, device_id={"head": lax.rem(head + o, n_head)}, device_id_type=MESH
        )

    q_copy = pltpu.make_async_copy(q_hbm, q_ref.at[:, :width], loc_sem.at[0])
    q_copy.start()
    k_copy = pltpu.make_async_copy(k_hbm, kbuf.at[rank], loc_sem.at[1])
    k_copy.start()
    mass[...] = jnp.zeros_like(mass)
    pool[...] = jnp.zeros_like(pool)
    if safe:
        peak[...] = jnp.full_like(peak, NEG_FLOOR)
    k_copy.wait()
    pl.semaphore_wait(barrier, n_ctx + n_head - 2)

    def key_copy(piece, to, sem):
        return pltpu.make_async_remote_copy(
            src_ref=kbuf.at[piece],
            dst_ref=kbuf.at[piece],
            send_sem=sem,
            recv_sem=key_recv.at[piece],
            device_id={"ctx": to},
            device_id_type=MESH,
        )

    z_next = lax.rem(zee + 1, n_z)
    z_prev = lax.rem(zee + n_z - 1, n_z)
    z_far = lax.rem(zee + 2, n_z)
    to_next = plane + z_next * 2 + core
    to_prev = plane + z_prev * 2 + core
    own_sibling = key_copy(rank, sibling, own_send.at[0])
    own_next = key_copy(rank, to_next, own_send.at[1])
    own_prev = key_copy(rank, to_prev, own_send.at[2])
    own_up = key_copy(rank, partner, own_send.at[3])

    def lower(z):
        return z * 2 + core

    def higher(z):
        return half_ctx + z * 2 + core

    def to_sibling(piece):
        return key_copy(piece, sibling, fwd_send.at[piece])

    def onward(piece):
        return key_copy(piece, to_next, next_send.at[piece])

    def backward(piece):
        return key_copy(piece, to_prev, prev_send.at[piece])

    def arrived(piece):
        key_copy(piece, sibling, own_send.at[0]).wait_recv()

    q_ship = pltpu.make_async_remote_copy(
        src_ref=q_hbm.at[:, kept:],
        dst_ref=q_ref.at[:, width:],
        send_sem=q_sem.at[0],
        recv_sem=q_sem.at[1],
        device_id={"ctx": partner},
        device_id_type=MESH,
    )

    @pl.when(upper == 0)
    def _():
        own_up.start()
        own_prev.start()
        own_next.start()
        own_sibling.start()

    @pl.when(upper == 1)
    def _():
        q_ship.start()

        @pl.when(zee < n_z - 1)
        def _():
            own_next.start()

        @pl.when(zee == 0)
        def _():
            own_prev.start()

        @pl.when(core == 0)
        def _():
            own_sibling.start()

    q_copy.wait()

    def tile_sum(h, keys, row_low, row_count, mask):
        q = q_ref[pl.ds(row_low, row_count), pl.ds(pl.multiple_of(h * D_HEAD, D_HEAD), D_HEAD)]
        s = lax.dot_general(keys, q, NT, preferred_element_type=F32)
        if safe:
            shown = s if mask is None else jnp.where(mask, s, NEG_FLOOR)
            top = jnp.max(shown, axis=0, keepdims=True)
            s = s - top
        else:
            top = None
        p = jnp.exp2(s * EXP2_SCALE)
        if mask is not None:
            p = jnp.where(mask, p, 0.0)
        return jnp.sum(p, axis=0, keepdims=True), top

    def put(h, block, low, count, value):
        mass[h, pl.ds(block, 1), pl.ds(low, count)] = value[0]
        if safe:
            peak[h, pl.ds(block, 1), pl.ds(low, count)] = value[1]

    def pool_of(keys):
        return jnp.sum(keys.astype(F32), axis=0, keepdims=True) * (1.0 / BLOCK)

    own_block = rank * 2
    sub = BLOCK // 2
    tri_wide = lax.broadcasted_iota(jnp.int32, (sub, BLOCK), 0) <= lax.broadcasted_iota(
        jnp.int32, (sub, BLOCK), 1
    )
    tri = tri_wide[:, :sub]

    def diagonal(h, keys, block, low):
        early = tile_sum(h, keys[:sub], low, BLOCK, tri_wide)
        late = tile_sum(h, keys[sub:], low + sub, sub, tri)
        put(h, block, low, sub, tuple(None if x is None else x[:, :sub] for x in early))
        both = early[0][:, sub:] + late[0]
        top = early[1]
        if safe:
            top = jnp.maximum(early[1][:, sub:], late[1])
            both = early[0][:, sub:] * jnp.exp2((early[1][:, sub:] - top) * EXP2_SCALE) + late[
                0
            ] * jnp.exp2((late[1] - top) * EXP2_SCALE)
        put(h, block, low + sub, sub, (both, top))

    first = kbuf[rank, :BLOCK]
    second = kbuf[rank, BLOCK:]
    pool[pl.ds(own_block, 1), :] = pool_of(first)
    pool[pl.ds(own_block + 1, 1), :] = pool_of(second)
    for h in range(GROUP):
        diagonal(h, first, own_block, 0)
        put(h, own_block, BLOCK, BLOCK, tile_sum(h, first, BLOCK, BLOCK, None))
        diagonal(h, second, own_block + 1, BLOCK)

    def ship_copy(z):
        return pltpu.make_async_remote_copy(
            src_ref=ship_out.at[z],
            dst_ref=ship_in.at[z],
            send_sem=ship_send.at[z],
            recv_sem=ship_recv.at[z],
            device_id={"ctx": partner},
            device_id_type=MESH,
        )

    def pick(i, values):
        out = values[-1]
        for n in range(len(values) - 2, -1, -1):
            out = jnp.where(i == n, values[n], out)
        return out

    shapes = [(j, blk, part) for j in range(2) for blk in range(4) for part in range(2)]
    kept_state = (mass, peak) if safe else (mass,)
    n_steps = 11

    def step(i, _):
        low = upper == 0
        high = upper == 1

        @pl.when(low & (i == 1))
        def _():
            arrived(lower(z_next))
            backward(lower(z_next)).start()
            to_sibling(lower(z_next)).start()
            arrived(lower(z_prev))
            to_sibling(lower(z_prev)).start()

        @pl.when(low & (i == 5))
        def _():
            q_ship.wait_recv()

        @pl.when(low & (i == 7))
        def _():
            arrived(lower(z_far))
            to_sibling(lower(z_far)).start()

        @pl.when(high & (i == 1))
        def _():
            @pl.when(zee > 0)
            def _():
                arrived(higher(z_prev))

                @pl.when(zee < n_z - 1)
                def _():
                    onward(higher(z_prev)).start()

                to_sibling(higher(z_prev)).start()

            arrived(lower(zee))
            backward(lower(zee)).start()
            onward(lower(zee)).start()
            to_sibling(lower(zee)).start()

        @pl.when(high & (i == 3) & (zee == n_z - 1))
        def _():
            arrived(higher(0))
            to_sibling(higher(0)).start()

        @pl.when(high & (i == 5))
        def _():
            arrived(lower(z_next))
            backward(lower(z_next)).start()
            to_sibling(lower(z_next)).start()

            @pl.when(zee >= 2)
            def _():
                arrived(higher(z_far))
                to_sibling(higher(z_far)).start()

        @pl.when(high & (i == 7))
        def _():
            arrived(lower(z_prev))
            to_sibling(lower(z_prev)).start()

        @pl.when(high & (i == 9))
        def _():
            arrived(lower(z_far))
            to_sibling(lower(z_far)).start()

        phase = lax.rem(i + 1, 2)
        narrow = jnp.where(low, (i < 5) | (i > 8), i < 7)
        lo_z = pick(
            i, (zee, z_prev, z_prev, z_next, z_next, zee, z_prev, z_next, z_far, z_far, z_far)
        )
        hi_z = pick(i, (zee, z_prev, z_prev, 0, 0, z_far, z_far, zee, z_prev, z_next, z_far))
        here = jnp.where(low, lo_z, hi_z)
        lo_side = jnp.where(i == 9, core, 1 - core)
        side = jnp.where(phase == 0, core, 1 - core)
        side = jnp.where(low & (i > 8), lo_side, side)
        piece = jnp.where(high & narrow, half_ctx, 0) + here * 2 + side
        least = pick(i, (0, 1, 1, 3, 3, 2, 2, 0, 0, 0, 0))
        live = jnp.where(
            low,
            piece < rank,
            jnp.where(i == 0, core == 1, zee >= least),
        )
        lo_wait = (i == 0) | (i == 2) | (i == 4) | (i == 8)
        hi_wait = (i >= 7) | (live & (phase == 1))
        wait = jnp.where(low, lo_wait, hi_wait)

        @pl.when(wait)
        def _():
            arrived(jnp.where(narrow, piece, here * 2 + 1 - core))

        @pl.when(narrow & live)
        def _():
            for half in range(2):
                keys = kbuf[piece, half * BLOCK : (half + 1) * BLOCK]
                block = piece * 2 + half
                pool[pl.ds(block, 1), :] = pool_of(keys)
                for h in range(GROUP):
                    put(h, block, 0, rows, tile_sum(h, keys, 0, rows, None))

        @pl.when(jnp.logical_not(narrow))
        def _():
            base = jnp.where(low, GROUP, 0)
            for blk in range(4):
                keys = kbuf[here * 2 + blk // 2, blk % 2 * BLOCK : (blk % 2 + 1) * BLOCK]
                block = here * 4 + blk
                pool[pl.ds(block, 1), :] = pool_of(keys)
                for j in range(2):
                    put(base + j, block, 0, rows, tile_sum(base + j, keys, 0, rows, None))

        @pl.when(low & jnp.logical_not(narrow))
        def _():
            for k, source in enumerate(kept_state):
                for n, (j, blk, part) in enumerate(shapes):
                    ship_out[here, k * 16 + n, :] = source[
                        GROUP + j, here * 4 + blk, part * BLOCK : (part + 1) * BLOCK
                    ]
            ship_copy(here).start()

        return 0

    lax.fori_loop(0, n_steps, step, 0)

    def collect():
        def one(z, _):
            ship_copy(z).wait_recv()
            for k, target in enumerate(kept_state):
                for n, (j, blk, part) in enumerate(shapes):
                    target[2 + j, z * 4 + blk, part * BLOCK : (part + 1) * BLOCK] = ship_in[
                        z, k * 16 + n, :
                    ]
            return 0

        lax.fori_loop(0, n_z, one, 0)

    p1, p2, p3 = split3(pool[...])
    pool_rows = jnp.concatenate([p1, p2, p3], axis=0)
    pool_stack = jnp.concatenate([p1, p2, p3, p1, p2, p1], axis=0)
    block_id = lax.broadcasted_iota(jnp.int32, (n_block, rows), 0)
    row_block = own_block + lax.broadcasted_iota(jnp.int32, (n_block, rows), 1) // BLOCK
    allowed = block_id <= row_block
    grad_sum = jnp.zeros((n_block, D_HEAD), F32)
    entropy = jnp.zeros((1, rows), F32)
    bad = jnp.zeros((1, rows), F32)
    for h in range(GROUP):
        if h == 2:
            pl.when(upper == 1)(collect)
        q = q_ref[:, h * D_HEAD : (h + 1) * D_HEAD]
        g3 = lax.dot_general(pool_rows, q, NT, preferred_element_type=F32)
        logits = (g3[2 * n_block :] + g3[n_block : 2 * n_block]) + g3[:n_block]
        m = mass[h]
        if safe:
            top = jnp.max(peak[h], axis=0, keepdims=True)
            m = m * jnp.exp2((peak[h] - top) * EXP2_SCALE)
        total = jnp.sum(m, axis=0, keepdims=True)
        fine = (total > TOTAL_LOW) & (total < TOTAL_HIGH)
        bad = bad + jnp.where(fine, 0.0, 1.0)
        teacher = m / total
        top = jnp.max(jnp.where(allowed, logits, NEG_FLOOR), axis=0, keepdims=True)
        weights = jnp.where(allowed, jnp.exp(logits - top), 0.0)
        weight_sum = jnp.sum(weights, axis=0, keepdims=True)
        student = weights / weight_sum
        entropy = entropy + (
            top + jnp.log(weight_sum) - jnp.sum(teacher * logits, axis=0, keepdims=True)
        )
        e1, e2, e3 = split3(student - teacher)
        three = jnp.concatenate([e1, e2, e3], axis=0)
        parts[h] = three
        g = lax.dot_general(three, q, NN, preferred_element_type=F32)
        grad_sum = grad_sum + ((g[2 * n_block :] + g[n_block : 2 * n_block]) + g[:n_block])

    grad_sum = grad_sum * (1.0 / BLOCK)
    lane_sum = lambda x: sum(x[:, i * 128 : (i + 1) * 128] for i in range(rows // 128))
    entropy_lanes = lane_sum(entropy)
    bad_lanes = lane_sum(bad)
    for t in range(n_ctx):
        gbs[t, 0:2, :] = grad_sum[2 * t : 2 * t + 2, :]
        gbs[t, 2:3, :] = entropy_lanes
        gbs[t, 3:4, :] = bad_lanes
        gbs[t, 4:8, :] = jnp.zeros((4, 128), F32)

    def r1_copy(slot, to):
        return pltpu.make_async_remote_copy(
            src_ref=gbs.at[to],
            dst_ref=gbr.at[slot],
            send_sem=r1_send.at[to],
            recv_sem=r1_recv.at[slot],
            device_id={"ctx": to},
            device_id_type=MESH,
        )

    @pl.loop(1, n_ctx)
    def _(o):
        r1_copy(rank, lax.rem(rank + o, n_ctx)).start()

    gbr[rank] = gbs[rank]

    def grad_rows(h):
        e1 = parts[h, :n_block]
        e2 = parts[h, n_block : 2 * n_block]
        e3 = parts[h, 2 * n_block :]
        stack = jnp.concatenate([e1, e1, e1, e2, e2, e3], axis=0)
        gq_ref[:, h * D_HEAD : (h + 1) * D_HEAD] = lax.dot_general(
            stack, pool_stack, TN, preferred_element_type=F32
        )

    for h in range(GROUP):
        grad_rows(h)

    @pl.loop(1, n_ctx)
    def _(o):
        other = lax.rem(rank + o, n_ctx)
        r1_copy(other, other).wait_recv()

    whole = gbr[0]
    for t in range(1, n_ctx):
        whole = whole + gbr[t]
    gb_ref[...] = whole[0:2]
    hsend[...] = whole

    def r2_copy(slot, to):
        return pltpu.make_async_remote_copy(
            src_ref=hsend,
            dst_ref=hrecv.at[slot],
            send_sem=r2_send.at[to],
            recv_sem=r2_recv.at[slot],
            device_id={"head": to},
            device_id_type=MESH,
        )

    @pl.loop(1, n_head)
    def _(o):
        r2_copy(head, lax.rem(head + o, n_head)).start()

    hrecv[head] = whole

    @pl.loop(1, n_ctx)
    def _(o):
        other = lax.rem(rank + o, n_ctx)
        r1_copy(rank, other).wait_send()

    @pl.when(upper == 0)
    def _():
        for own in (own_sibling, own_next, own_prev, own_up):
            own.wait_send()
        backward(lower(z_next)).wait_send()
        for z in (z_prev, z_next, z_far):
            to_sibling(lower(z)).wait_send()
        for z in range(n_z):
            ship_copy(z).wait_send()

    @pl.when(upper == 1)
    def _():
        q_ship.wait_send()
        backward(lower(zee)).wait_send()
        onward(lower(zee)).wait_send()
        backward(lower(z_next)).wait_send()
        for z in range(n_z):
            to_sibling(lower(z)).wait_send()

        @pl.when(core == 0)
        def _():
            own_sibling.wait_send()

        @pl.when(zee < n_z - 1)
        def _():
            own_next.wait_send()

        @pl.when(zee == 0)
        def _():
            own_prev.wait_send()

        @pl.when((zee > 0) & (zee < n_z - 1))
        def _():
            onward(higher(z_prev)).wait_send()

        @pl.loop(0, zee)
        def _(z):
            to_sibling(higher(z)).wait_send()

    @pl.loop(1, n_head)
    def _(o):
        other = lax.rem(head + o, n_head)
        r2_copy(other, other).wait_recv()

    final = hrecv[0]
    for t in range(1, n_head):
        final = final + hrecv[t]
    sums = jnp.sum(final, axis=1, keepdims=True)
    loss_ref[...] = sums[2:3] * (1.0 / (rows * n_ctx * HEADS))
    bad_ref[...] = sums[3:4]

    @pl.loop(1, n_head)
    def _(o):
        other = lax.rem(head + o, n_head)
        r2_copy(head, other).wait_send()


def run(safe, n_ctx, n_head, queries, keys):
    rows = queries.shape[0]
    n_block = n_ctx * rows // BLOCK
    half_ctx = n_ctx // 2
    ship_rows = 32 if safe else 16
    dma = pltpu.SemaphoreType.DMA
    return pl.pallas_call(
        functools.partial(kernel, safe, n_ctx, n_head),
        out_shape=(
            jax.ShapeDtypeStruct((rows, GROUP * D_HEAD), F32),
            jax.ShapeDtypeStruct((rows // BLOCK, D_HEAD), F32),
            jax.ShapeDtypeStruct((1, 1), F32),
            jax.ShapeDtypeStruct((1, 1), F32),
        ),
        in_specs=[pl.BlockSpec(memory_space=pl.ANY)] * 2,
        out_specs=(pl.BlockSpec(memory_space=pltpu.VMEM),) * 4,
        scratch_shapes=[
            pltpu.VMEM((rows, (GROUP + 2) * D_HEAD), BF16),
            pltpu.VMEM((n_ctx, rows, D_HEAD), BF16),
            pltpu.VMEM((GROUP + 2, n_block, rows), F32),
            pltpu.VMEM((GROUP + 2, n_block, rows) if safe else (8, 128), F32),
            pltpu.VMEM((n_block, D_HEAD), F32),
            pltpu.VMEM((GROUP, 3 * n_block, rows), BF16),
            pltpu.VMEM((half_ctx // 2, ship_rows, BLOCK), F32),
            pltpu.VMEM((half_ctx // 2, ship_rows, BLOCK), F32),
            pltpu.VMEM((n_ctx, 8, 128), F32),
            pltpu.VMEM((n_ctx, 8, 128), F32),
            pltpu.VMEM((8, 128), F32),
            pltpu.VMEM((n_head, 8, 128), F32),
            dma((2,)),
            dma((2,)),
            dma((4,)),
            dma((n_ctx,)),
            dma((n_ctx,)),
            dma((n_ctx,)),
            dma((n_ctx,)),
            dma((half_ctx,)),
            dma((half_ctx,)),
            dma((n_ctx,)),
            dma((n_ctx,)),
            dma((n_head,)),
            dma((n_head,)),
        ],
        compiler_params=pltpu.CompilerParams(
            collective_id=1 if safe else 0,
            has_side_effects=True,
            vmem_limit_bytes=48 * 1024 * 1024,
        ),
        name="gate_safe" if safe else "gate_fast",
    )(queries, keys)


def solution(mesh):
    n_ctx, n_head = mesh.shape["ctx"], mesh.shape["head"]

    def local(queries, keys):
        fast = run(False, n_ctx, n_head, queries, keys)
        ok = fast[3].reshape(()) == 0.0
        out = lax.cond(
            ok,
            lambda: fast[:3],
            lambda: run(True, n_ctx, n_head, queries, keys)[:3],
        )
        return out[0], out[1], out[2].reshape(())

    return jax.shard_map(
        local,
        mesh=mesh,
        in_specs=(P("ctx", "head"), P("ctx", "head")),
        out_specs=(P("ctx", "head"), P("ctx", "head"), P()),
        check_vma=False,
    )
```

```python
import functools
import math

import jax
import jax.numpy as jnp
from jax import lax
from jax.experimental import pallas as pl
from jax.experimental.pallas import tpu as pltpu
from jax.sharding import PartitionSpec as P

D_HEAD = 128
HEADS = 32
KV_HEADS = 8
BLOCK = 512
GROUP = HEADS // KV_HEADS
NEG_FLOOR = -1e30
SCALE = D_HEAD ** (-0.5)
EXP2_SCALE = SCALE * math.log2(math.e)
TOTAL_LOW = 1e-25
TOTAL_HIGH = 3e38
MESH = pl.DeviceIdType.MESH
NT = (((1,), (1,)), ((), ()))
NN = (((1,), (0,)), ((), ()))
TN = (((0,), (0,)), ((), ()))
F32 = jnp.float32
BF16 = jnp.bfloat16


def split3(x):
    a = x.astype(BF16)
    rest = x - a.astype(F32)
    b = rest.astype(BF16)
    c = (rest - b.astype(F32)).astype(BF16)
    return a, b, c


def kernel(
    safe,
    n_ctx,
    n_head,
    q_hbm,
    k_hbm,
    gq_ref,
    gb_ref,
    loss_ref,
    bad_ref,
    q_ref,
    kbuf,
    mass,
    peak,
    pool,
    parts,
    ship_out,
    ship_in,
    gbs,
    gbr,
    hsend,
    hrecv,
    loc_sem,
    q_sem,
    own_send,
    fwd_send,
    next_send,
    prev_send,
    key_recv,
    ship_send,
    ship_recv,
    zq_sem,
    r1_send,
    r1_recv,
    r2_send,
    r2_recv,
):
    rank = lax.axis_index("ctx")
    head = lax.axis_index("head")
    half_ctx = n_ctx // 2
    n_z = half_ctx // 2
    upper = rank // half_ctx
    zee = lax.rem(rank, half_ctx) // 2
    core = lax.rem(rank, 2)
    plane = upper * half_ctx
    sibling = plane + zee * 2 + 1 - core
    partner = lax.rem(rank + half_ctx, n_ctx)
    rows = mass.shape[2]
    n_block = mass.shape[1]
    width = GROUP * D_HEAD
    kept = width // 2

    barrier = pltpu.get_barrier_semaphore()

    @pl.loop(1, n_ctx)
    def _(o):
        pl.semaphore_signal(
            barrier, inc=1, device_id={"ctx": lax.rem(rank + o, n_ctx)}, device_id_type=MESH
        )

    @pl.loop(1, n_head)
    def _(o):
        pl.semaphore_signal(
            barrier, inc=1, device_id={"head": lax.rem(head + o, n_head)}, device_id_type=MESH
        )

    q_copy = pltpu.make_async_copy(q_hbm, q_ref.at[:, :width], loc_sem.at[0])
    q_copy.start()
    k_copy = pltpu.make_async_copy(k_hbm, kbuf.at[rank], loc_sem.at[1])
    k_copy.start()
    mass[...] = jnp.zeros_like(mass)
    pool[...] = jnp.zeros_like(pool)
    if safe:
        peak[...] = jnp.full_like(peak, NEG_FLOOR)
    k_copy.wait()
    pl.semaphore_wait(barrier, n_ctx + n_head - 2)

    def key_copy(piece, to, sem):
        return pltpu.make_async_remote_copy(
            src_ref=kbuf.at[piece],
            dst_ref=kbuf.at[piece],
            send_sem=sem,
            recv_sem=key_recv.at[piece],
            device_id={"ctx": to},
            device_id_type=MESH,
        )

    z_next = lax.rem(zee + 1, n_z)
    z_prev = lax.rem(zee + n_z - 1, n_z)
    z_far = lax.rem(zee + 2, n_z)
    to_next = plane + z_next * 2 + core
    to_prev = plane + z_prev * 2 + core
    own_sibling = key_copy(rank, sibling, own_send.at[0])
    own_next = key_copy(rank, to_next, own_send.at[1])
    own_prev = key_copy(rank, to_prev, own_send.at[2])
    own_up = key_copy(rank, partner, own_send.at[3])

    def lower(z):
        return z * 2 + core

    def higher(z):
        return half_ctx + z * 2 + core

    def to_sibling(piece):
        return key_copy(piece, sibling, fwd_send.at[piece])

    def onward(piece):
        return key_copy(piece, to_next, next_send.at[piece])

    def backward(piece):
        return key_copy(piece, to_prev, prev_send.at[piece])

    def arrived(piece):
        key_copy(piece, sibling, own_send.at[0]).wait_recv()

    q_ship = pltpu.make_async_remote_copy(
        src_ref=q_hbm.at[:, kept:],
        dst_ref=q_ref.at[:, width : width + kept],
        send_sem=q_sem.at[0],
        recv_sem=q_sem.at[1],
        device_id={"ctx": partner},
        device_id_type=MESH,
    )

    z_mate = plane + (n_z - 1 - zee) * 2 + core
    z_first = zee == 0
    z_last = zee == n_z - 1
    zq_ship = pltpu.make_async_remote_copy(
        src_ref=q_hbm.at[:, kept:],
        dst_ref=q_ref.at[:, width + kept :],
        send_sem=zq_sem.at[0],
        recv_sem=zq_sem.at[1],
        device_id={"ctx": z_mate},
        device_id_type=MESH,
    )

    @pl.when(z_last)
    def _():
        zq_ship.start()

    @pl.when(upper == 0)
    def _():
        own_up.start()
        own_prev.start()
        own_next.start()
        own_sibling.start()

    @pl.when(upper == 1)
    def _():
        q_ship.start()

        @pl.when(zee < n_z - 1)
        def _():
            own_next.start()

        @pl.when(zee <= 1)
        def _():
            own_prev.start()

        @pl.when((core == 0) | z_first)
        def _():
            own_sibling.start()

    q_copy.wait()

    def tile_sum(h, keys, row_low, row_count, mask):
        q = q_ref[pl.ds(row_low, row_count), pl.ds(pl.multiple_of(h * D_HEAD, D_HEAD), D_HEAD)]
        s = lax.dot_general(keys, q, NT, preferred_element_type=F32)
        if safe:
            shown = s if mask is None else jnp.where(mask, s, NEG_FLOOR)
            top = jnp.max(shown, axis=0, keepdims=True)
            s = s - top
        else:
            top = None
        p = jnp.exp2(s * EXP2_SCALE)
        if mask is not None:
            p = jnp.where(mask, p, 0.0)
        return jnp.sum(p, axis=0, keepdims=True), top

    def put(h, block, low, count, value):
        mass[h, pl.ds(block, 1), pl.ds(low, count)] = value[0]
        if safe:
            peak[h, pl.ds(block, 1), pl.ds(low, count)] = value[1]

    def pool_of(keys):
        return jnp.sum(keys.astype(F32), axis=0, keepdims=True) * (1.0 / BLOCK)

    own_block = rank * 2
    sub = BLOCK // 2
    tri_wide = lax.broadcasted_iota(jnp.int32, (sub, BLOCK), 0) <= lax.broadcasted_iota(
        jnp.int32, (sub, BLOCK), 1
    )
    tri = tri_wide[:, :sub]

    def diagonal(h, keys, block, low):
        early = tile_sum(h, keys[:sub], low, BLOCK, tri_wide)
        late = tile_sum(h, keys[sub:], low + sub, sub, tri)
        put(h, block, low, sub, tuple(None if x is None else x[:, :sub] for x in early))
        both = early[0][:, sub:] + late[0]
        top = early[1]
        if safe:
            top = jnp.maximum(early[1][:, sub:], late[1])
            both = early[0][:, sub:] * jnp.exp2((early[1][:, sub:] - top) * EXP2_SCALE) + late[
                0
            ] * jnp.exp2((late[1] - top) * EXP2_SCALE)
        put(h, block, low + sub, sub, (both, top))

    first = kbuf[rank, :BLOCK]
    second = kbuf[rank, BLOCK:]
    pool[pl.ds(own_block, 1), :] = pool_of(first)
    pool[pl.ds(own_block + 1, 1), :] = pool_of(second)
    for h in range(GROUP):
        diagonal(h, first, own_block, 0)
        put(h, own_block, BLOCK, BLOCK, tile_sum(h, first, BLOCK, BLOCK, None))
        diagonal(h, second, own_block + 1, BLOCK)

    def ship_copy(z):
        return pltpu.make_async_remote_copy(
            src_ref=ship_out.at[z],
            dst_ref=ship_in.at[z],
            send_sem=ship_send.at[z],
            recv_sem=ship_recv.at[z],
            device_id={"ctx": jnp.where(z < n_z, partner, z_mate)},
            device_id_type=MESH,
        )

    def pick(i, values):
        out = values[-1]
        for n in range(len(values) - 2, -1, -1):
            out = jnp.where(i == n, values[n], out)
        return out

    shapes = [(j, blk, part) for j in range(2) for blk in range(4) for part in range(2)]
    kept_state = (mass, peak) if safe else (mass,)
    n_steps = 9

    def lower_sib(z):
        return z * 2 + 1 - core

    def higher_sib(z):
        return half_ctx + z * 2 + 1 - core

    def step(i, _):
        low = upper == 0
        high = upper == 1

        @pl.when(low)
        def _():
            @pl.when(i == 0)
            def _():
                arrived(sibling)

            @pl.when(i == 1)
            def _():
                arrived(lower(z_next))
                backward(lower(z_next)).start()
                to_sibling(lower(z_next)).start()

            @pl.when(i == jnp.where(z_first, 6, 1))
            def _():
                arrived(lower(z_prev))
                to_sibling(lower(z_prev)).start()

            @pl.when(i == jnp.where(z_first, 7, 2))
            def _():
                arrived(lower_sib(z_prev))

            @pl.when(i == 3)
            def _():
                arrived(lower_sib(z_next))

            @pl.when(i == jnp.where(z_last, 4, 3))
            def _():
                q_ship.wait_recv()

            @pl.when(i == 4)
            def _():
                arrived(lower(z_far))
                to_sibling(lower(z_far)).start()

            @pl.when(i == 5)
            def _():
                arrived(lower_sib(z_far))

        @pl.when(high)
        def _():
            @pl.when((i == 0) & (core == 1))
            def _():
                arrived(sibling)

            @pl.when(i == 1)
            def _():
                @pl.when(zee > 0)
                def _():
                    arrived(higher(z_prev))

                    @pl.when(zee < n_z - 1)
                    def _():
                        onward(higher(z_prev)).start()

                    to_sibling(higher(z_prev)).start()

                arrived(lower(zee))
                backward(lower(zee)).start()
                onward(lower(zee)).start()
                to_sibling(lower(zee)).start()

            @pl.when((i == 2) & (zee > 0))
            def _():
                arrived(higher_sib(z_prev))

            @pl.when((i == 2) & z_last)
            def _():
                arrived(higher(0))
                to_sibling(higher(0)).start()

            @pl.when(i == 3)
            def _():
                arrived(lower_sib(zee))

                @pl.when(z_last)
                def _():
                    arrived(higher_sib(0))

            @pl.when(i == 4)
            def _():
                arrived(lower(z_next))
                backward(lower(z_next)).start()
                to_sibling(lower(z_next)).start()

                @pl.when(zee >= 2)
                def _():
                    arrived(higher(z_far))
                    to_sibling(higher(z_far)).start()

                @pl.when(z_first)
                def _():
                    arrived(higher(1))
                    to_sibling(higher(1)).start()

            @pl.when((i == 5) & (zee >= 2))
            def _():
                arrived(higher_sib(z_far))

            @pl.when(i == 6)
            def _():
                arrived(lower_sib(z_next))
                arrived(lower(z_prev))
                to_sibling(lower(z_prev)).start()

            @pl.when(i == 7)
            def _():
                arrived(lower_sib(z_prev))
                arrived(lower(z_far))
                to_sibling(lower(z_far)).start()

            @pl.when(i == 8)
            def _():
                arrived(lower_sib(z_far))

            @pl.when((i == 4) & z_first & (core == 0))
            def _():
                arrived(sibling)

            @pl.when((i == 5) & z_first)
            def _():
                arrived(higher_sib(1))

        @pl.when((i == 4) & z_first)
        def _():
            zq_ship.wait_recv()

        narrow = (i <= 2) | ((zee == n_z - 2) & ((i == 4) | (i == 5)))
        side = jnp.where((i == 1) | (i == 4), core, 1 - core)
        piece = plane + pick(i, (zee, z_prev, z_prev, 0)) * 2 + side
        z_turn = z_first & ((i == 4) | (i == 5))
        own_turn = jnp.where(low, 8, 5)
        in_plane = z_turn | (z_last & ((i == 3) | (i == own_turn)))
        here = pick(
            i,
            (
                0,
                0,
                0,
                jnp.where(z_last, 0, zee),
                jnp.where(z_first, 0, zee),
                1,
                z_next,
                z_prev,
                z_far,
            ),
        )
        first_piece = jnp.where(in_plane, plane, 0) + here * 2
        base = jnp.where(
            z_turn, GROUP + 2, jnp.where(low & jnp.logical_not(in_plane), GROUP, 0)
        )
        live = jnp.where(
            i == 0,
            core == 1,
            (zee >= pick(i, (0, 1, 1, 0, 2, 2, 0, 0, 0))) | z_turn,
        )

        @pl.when(narrow & live)
        def _():
            for half in range(2):
                keys = kbuf[piece, half * BLOCK : (half + 1) * BLOCK]
                block = piece * 2 + half
                pool[pl.ds(block, 1), :] = pool_of(keys)
                for h in range(GROUP):
                    put(h, block, 0, rows, tile_sum(h, keys, 0, rows, None))

        @pl.when(jnp.logical_not(narrow) & live)
        def _():
            for blk in range(4):
                keys = kbuf[first_piece + blk // 2, blk % 2 * BLOCK : (blk % 2 + 1) * BLOCK]
                block = first_piece * 2 + blk
                pool[pl.ds(block, 1), :] = pool_of(keys)
                for j in range(2):
                    put(base + j, block, 0, rows, tile_sum(base + j, keys, 0, rows, None))

        @pl.when(live & jnp.logical_not(narrow) & (base > 0))
        def _():
            slot = jnp.where(z_turn, n_z, 0) + here
            for k, source in enumerate(kept_state):
                for n, (j, blk, part) in enumerate(shapes):
                    ship_out[slot, k * 16 + n, :] = source[
                        base + j, first_piece * 2 + blk, part * BLOCK : (part + 1) * BLOCK
                    ]
            ship_copy(slot).start()

        return 0

    lax.fori_loop(0, n_steps, step, 0)

    def collect(low_slot, high_slot, first_block):
        def one(z, _):
            ship_copy(z).wait_recv()
            for k, target in enumerate(kept_state):
                for n, (j, blk, part) in enumerate(shapes):
                    target[
                        2 + j,
                        first_block + (z - low_slot) * 4 + blk,
                        part * BLOCK : (part + 1) * BLOCK,
                    ] = ship_in[z, k * 16 + n, :]
            return 0

        lax.fori_loop(low_slot, high_slot, one, 0)

    p1, p2, p3 = split3(pool[...])
    pool_rows = jnp.concatenate([p1, p2, p3], axis=0)
    pool_stack = jnp.concatenate([p1, p2, p3, p1, p2, p1], axis=0)
    block_id = lax.broadcasted_iota(jnp.int32, (n_block, rows), 0)
    row_block = own_block + lax.broadcasted_iota(jnp.int32, (n_block, rows), 1) // BLOCK
    allowed = block_id <= row_block
    grad_sum = jnp.zeros((n_block, D_HEAD), F32)
    entropy = jnp.zeros((1, rows), F32)
    bad = jnp.zeros((1, rows), F32)
    for h in range(GROUP):
        if h == 2:
            pl.when(upper == 1)(functools.partial(collect, 0, n_z, 0))
            pl.when(z_last)(functools.partial(collect, n_z, n_z + 2, plane * 2))
        q = q_ref[:, h * D_HEAD : (h + 1) * D_HEAD]
        g3 = lax.dot_general(pool_rows, q, NT, preferred_element_type=F32)
        logits = (g3[2 * n_block :] + g3[n_block : 2 * n_block]) + g3[:n_block]
        m = mass[h]
        if safe:
            top = jnp.max(peak[h], axis=0, keepdims=True)
            m = m * jnp.exp2((peak[h] - top) * EXP2_SCALE)
        total = jnp.sum(m, axis=0, keepdims=True)
        fine = (total > TOTAL_LOW) & (total < TOTAL_HIGH)
        bad = bad + jnp.where(fine, 0.0, 1.0)
        teacher = m / total
        top = jnp.max(jnp.where(allowed, logits, NEG_FLOOR), axis=0, keepdims=True)
        weights = jnp.where(allowed, jnp.exp(logits - top), 0.0)
        weight_sum = jnp.sum(weights, axis=0, keepdims=True)
        student = weights / weight_sum
        entropy = entropy + (
            top + jnp.log(weight_sum) - jnp.sum(teacher * logits, axis=0, keepdims=True)
        )
        e1, e2, e3 = split3(student - teacher)
        three = jnp.concatenate([e1, e2, e3], axis=0)
        parts[h] = three
        g = lax.dot_general(three, q, NN, preferred_element_type=F32)
        grad_sum = grad_sum + ((g[2 * n_block :] + g[n_block : 2 * n_block]) + g[:n_block])

    grad_sum = grad_sum * (1.0 / BLOCK)
    lane_sum = lambda x: sum(x[:, i * 128 : (i + 1) * 128] for i in range(rows // 128))
    entropy_lanes = lane_sum(entropy)
    bad_lanes = lane_sum(bad)
    for t in range(n_ctx):
        gbs[t, 0:2, :] = grad_sum[2 * t : 2 * t + 2, :]
        gbs[t, 2:3, :] = entropy_lanes
        gbs[t, 3:4, :] = bad_lanes
        gbs[t, 4:8, :] = jnp.zeros((4, 128), F32)

    def r1_copy(slot, to):
        return pltpu.make_async_remote_copy(
            src_ref=gbs.at[to],
            dst_ref=gbr.at[slot],
            send_sem=r1_send.at[to],
            recv_sem=r1_recv.at[slot],
            device_id={"ctx": to},
            device_id_type=MESH,
        )

    @pl.loop(1, n_ctx)
    def _(o):
        r1_copy(rank, lax.rem(rank + o, n_ctx)).start()

    gbr[rank] = gbs[rank]

    def grad_rows(h):
        e1 = parts[h, :n_block]
        e2 = parts[h, n_block : 2 * n_block]
        e3 = parts[h, 2 * n_block :]
        stack = jnp.concatenate([e1, e1, e1, e2, e2, e3], axis=0)
        gq_ref[:, h * D_HEAD : (h + 1) * D_HEAD] = lax.dot_general(
            stack, pool_stack, TN, preferred_element_type=F32
        )

    for h in range(GROUP):
        grad_rows(h)

    @pl.loop(1, n_ctx)
    def _(o):
        other = lax.rem(rank + o, n_ctx)
        r1_copy(other, other).wait_recv()

    whole = gbr[0]
    for t in range(1, n_ctx):
        whole = whole + gbr[t]
    gb_ref[...] = whole[0:2]
    hsend[...] = whole

    def r2_copy(slot, to):
        return pltpu.make_async_remote_copy(
            src_ref=hsend,
            dst_ref=hrecv.at[slot],
            send_sem=r2_send.at[to],
            recv_sem=r2_recv.at[slot],
            device_id={"head": to},
            device_id_type=MESH,
        )

    @pl.loop(1, n_head)
    def _(o):
        r2_copy(head, lax.rem(head + o, n_head)).start()

    hrecv[head] = whole

    @pl.loop(1, n_ctx)
    def _(o):
        r1_copy(rank, lax.rem(rank + o, n_ctx)).wait_send()

    @pl.when(upper == 0)
    def _():
        for own in (own_sibling, own_next, own_prev, own_up):
            own.wait_send()
        backward(lower(z_next)).wait_send()
        for z in (z_prev, z_next, z_far):
            to_sibling(lower(z)).wait_send()
        for z in range(n_z):
            ship_copy(z).wait_send()

    @pl.when(upper == 1)
    def _():
        q_ship.wait_send()
        backward(lower(zee)).wait_send()
        onward(lower(zee)).wait_send()
        backward(lower(z_next)).wait_send()
        for z in range(n_z):
            to_sibling(lower(z)).wait_send()

        @pl.when((core == 0) | z_first)
        def _():
            own_sibling.wait_send()

        @pl.when(zee < n_z - 1)
        def _():
            own_next.wait_send()

        @pl.when(zee <= 1)
        def _():
            own_prev.wait_send()

        @pl.when(z_first)
        def _():
            to_sibling(higher(1)).wait_send()

        @pl.when((zee > 0) & (zee < n_z - 1))
        def _():
            onward(higher(z_prev)).wait_send()

        @pl.loop(0, zee)
        def _(z):
            to_sibling(higher(z)).wait_send()

    @pl.when(z_last)
    def _():
        zq_ship.wait_send()

    @pl.when(z_first)
    def _():
        for z in range(n_z, n_z + 2):
            ship_copy(z).wait_send()

    @pl.loop(1, n_head)
    def _(o):
        other = lax.rem(head + o, n_head)
        r2_copy(other, other).wait_recv()

    final = hrecv[0]
    for t in range(1, n_head):
        final = final + hrecv[t]
    sums = jnp.sum(final, axis=1, keepdims=True)
    loss_ref[...] = sums[2:3] * (1.0 / (rows * n_ctx * HEADS))
    bad_ref[...] = sums[3:4]

    @pl.loop(1, n_head)
    def _(o):
        other = lax.rem(head + o, n_head)
        r2_copy(head, other).wait_send()


def run(safe, n_ctx, n_head, queries, keys):
    rows = queries.shape[0]
    n_block = n_ctx * rows // BLOCK
    half_ctx = n_ctx // 2
    ship_rows = 32 if safe else 16
    dma = pltpu.SemaphoreType.DMA
    return pl.pallas_call(
        functools.partial(kernel, safe, n_ctx, n_head),
        out_shape=(
            jax.ShapeDtypeStruct((rows, GROUP * D_HEAD), F32),
            jax.ShapeDtypeStruct((rows // BLOCK, D_HEAD), F32),
            jax.ShapeDtypeStruct((1, 1), F32),
            jax.ShapeDtypeStruct((1, 1), F32),
        ),
        in_specs=[pl.BlockSpec(memory_space=pl.ANY)] * 2,
        out_specs=(pl.BlockSpec(memory_space=pltpu.VMEM),) * 4,
        scratch_shapes=[
            pltpu.VMEM((rows, (GROUP + 4) * D_HEAD), BF16),
            pltpu.VMEM((n_ctx, rows, D_HEAD), BF16),
            pltpu.VMEM((GROUP + 4, n_block, rows), F32),
            pltpu.VMEM((GROUP + 4, n_block, rows) if safe else (8, 128), F32),
            pltpu.VMEM((n_block, D_HEAD), F32),
            pltpu.VMEM((GROUP, 3 * n_block, rows), BF16),
            pltpu.VMEM((half_ctx // 2 + 2, ship_rows, BLOCK), F32),
            pltpu.VMEM((half_ctx // 2 + 2, ship_rows, BLOCK), F32),
            pltpu.VMEM((n_ctx, 8, 128), F32),
            pltpu.VMEM((n_ctx, 8, 128), F32),
            pltpu.VMEM((8, 128), F32),
            pltpu.VMEM((n_head, 8, 128), F32),
            dma((2,)),
            dma((2,)),
            dma((4,)),
            dma((n_ctx,)),
            dma((n_ctx,)),
            dma((n_ctx,)),
            dma((n_ctx,)),
            dma((half_ctx,)),
            dma((half_ctx,)),
            dma((2,)),
            dma((n_ctx,)),
            dma((n_ctx,)),
            dma((n_head,)),
            dma((n_head,)),
        ],
        compiler_params=pltpu.CompilerParams(
            collective_id=1 if safe else 0,
            has_side_effects=True,
            vmem_limit_bytes=48 * 1024 * 1024,
        ),
        name="gate_safe" if safe else "gate_fast",
    )(queries, keys)


def solution(mesh):
    n_ctx, n_head = mesh.shape["ctx"], mesh.shape["head"]

    def local(queries, keys):
        fast = run(False, n_ctx, n_head, queries, keys)
        ok = fast[3].reshape(()) == 0.0
        out = lax.cond(
            ok,
            lambda: fast[:3],
            lambda: run(True, n_ctx, n_head, queries, keys)[:3],
        )
        return out[0], out[1], out[2].reshape(())

    return jax.shard_map(
        local,
        mesh=mesh,
        in_specs=(P("ctx", "head"), P("ctx", "head")),
        out_specs=(P("ctx", "head"), P("ctx", "head"), P()),
        check_vma=False,
    )
```

```python
import functools
import math

import jax
import jax.numpy as jnp
from jax import lax
from jax.experimental import pallas as pl
from jax.experimental.pallas import tpu as pltpu
from jax.sharding import PartitionSpec as P

D_HEAD = 128
HEADS = 32
KV_HEADS = 8
BLOCK = 512
GROUP = HEADS // KV_HEADS
NEG_FLOOR = -1e30
SCALE = D_HEAD ** (-0.5)
EXP2_SCALE = SCALE * math.log2(math.e)
TOTAL_LOW = 1e-25
TOTAL_HIGH = 3e38
MESH = pl.DeviceIdType.MESH
NT = (((1,), (1,)), ((), ()))
NN = (((1,), (0,)), ((), ()))
TN = (((0,), (0,)), ((), ()))
F32 = jnp.float32
BF16 = jnp.bfloat16


def split3(x):
    a = x.astype(BF16)
    rest = x - a.astype(F32)
    b = rest.astype(BF16)
    c = (rest - b.astype(F32)).astype(BF16)
    return a, b, c


def kernel(
    safe,
    n_ctx,
    n_head,
    q_hbm,
    k_hbm,
    gq_ref,
    gb_ref,
    loss_ref,
    bad_ref,
    q_ref,
    kbuf,
    mass,
    peak,
    pool,
    parts,
    ship_out,
    ship_in,
    gbs,
    gbr,
    hsend,
    hrecv,
    loc_sem,
    q_sem,
    own_send,
    fwd_send,
    next_send,
    prev_send,
    key_recv,
    ship_send,
    ship_recv,
    zq_sem,
    r1_send,
    r1_recv,
    r2_send,
    r2_recv,
):
    rank = lax.axis_index("ctx")
    head = lax.axis_index("head")
    half_ctx = n_ctx // 2
    n_z = half_ctx // 2
    upper = rank // half_ctx
    zee = lax.rem(rank, half_ctx) // 2
    core = lax.rem(rank, 2)
    plane = upper * half_ctx
    sibling = plane + zee * 2 + 1 - core
    partner = lax.rem(rank + half_ctx, n_ctx)
    rows = mass.shape[2]
    n_block = mass.shape[1]
    width = GROUP * D_HEAD
    kept = width // 2

    barrier = pltpu.get_barrier_semaphore()

    @pl.loop(1, n_ctx)
    def _(o):
        pl.semaphore_signal(
            barrier, inc=1, device_id={"ctx": lax.rem(rank + o, n_ctx)}, device_id_type=MESH
        )

    @pl.loop(1, n_head)
    def _(o):
        pl.semaphore_signal(
            barrier, inc=1, device_id={"head": lax.rem(head + o, n_head)}, device_id_type=MESH
        )

    q_copy = pltpu.make_async_copy(q_hbm, q_ref.at[:, :width], loc_sem.at[0])
    q_copy.start()
    k_copy = pltpu.make_async_copy(k_hbm, kbuf.at[rank], loc_sem.at[1])
    k_copy.start()
    mass[...] = jnp.zeros_like(mass)
    pool[...] = jnp.zeros_like(pool)
    if safe:
        peak[...] = jnp.full_like(peak, NEG_FLOOR)
    k_copy.wait()
    pl.semaphore_wait(barrier, n_ctx + n_head - 2)

    def key_copy(piece, to, sem):
        return pltpu.make_async_remote_copy(
            src_ref=kbuf.at[piece],
            dst_ref=kbuf.at[piece],
            send_sem=sem,
            recv_sem=key_recv.at[piece],
            device_id={"ctx": to},
            device_id_type=MESH,
        )

    z_next = lax.rem(zee + 1, n_z)
    z_prev = lax.rem(zee + n_z - 1, n_z)
    z_far = lax.rem(zee + 2, n_z)
    to_next = plane + z_next * 2 + core
    to_prev = plane + z_prev * 2 + core
    own_sibling = key_copy(rank, sibling, own_send.at[0])
    own_next = key_copy(rank, to_next, own_send.at[1])
    own_prev = key_copy(rank, to_prev, own_send.at[2])
    own_up = key_copy(rank, partner, own_send.at[3])

    def lower(z):
        return z * 2 + core

    def higher(z):
        return half_ctx + z * 2 + core

    def to_sibling(piece):
        return key_copy(piece, sibling, fwd_send.at[piece])

    def onward(piece):
        return key_copy(piece, to_next, next_send.at[piece])

    def backward(piece):
        return key_copy(piece, to_prev, prev_send.at[piece])

    def arrived(piece):
        key_copy(piece, sibling, own_send.at[0]).wait_recv()

    q_ship = pltpu.make_async_remote_copy(
        src_ref=q_hbm.at[:, kept:],
        dst_ref=q_ref.at[:, width : width + kept],
        send_sem=q_sem.at[0],
        recv_sem=q_sem.at[1],
        device_id={"ctx": partner},
        device_id_type=MESH,
    )

    z_mate = plane + (n_z - 1 - zee) * 2 + core
    z_first = zee == 0
    z_last = zee == n_z - 1
    zq_ship = pltpu.make_async_remote_copy(
        src_ref=q_hbm.at[:, kept:],
        dst_ref=q_ref.at[:, width + kept :],
        send_sem=zq_sem.at[0],
        recv_sem=zq_sem.at[1],
        device_id={"ctx": z_mate},
        device_id_type=MESH,
    )

    @pl.when(z_last)
    def _():
        zq_ship.start()

    @pl.when(upper == 0)
    def _():
        own_up.start()
        own_prev.start()
        own_next.start()
        own_sibling.start()

    @pl.when(upper == 1)
    def _():
        q_ship.start()

        @pl.when(zee < n_z - 1)
        def _():
            own_next.start()

        @pl.when(zee <= 1)
        def _():
            own_prev.start()

        @pl.when((core == 0) | z_first)
        def _():
            own_sibling.start()

    q_copy.wait()

    def tile_sum(h, keys, row_low, row_count, mask):
        q = q_ref[pl.ds(row_low, row_count), pl.ds(pl.multiple_of(h * D_HEAD, D_HEAD), D_HEAD)]
        s = lax.dot_general(keys, q, NT, preferred_element_type=F32)
        if safe:
            shown = s if mask is None else jnp.where(mask, s, NEG_FLOOR)
            top = jnp.max(shown, axis=0, keepdims=True)
            s = s - top
        else:
            top = None
        p = jnp.exp2(s * EXP2_SCALE)
        if mask is not None:
            p = jnp.where(mask, p, 0.0)
        return jnp.sum(p, axis=0, keepdims=True), top

    def put(h, block, low, count, value):
        mass[h, pl.ds(block, 1), pl.ds(low, count)] = value[0]
        if safe:
            peak[h, pl.ds(block, 1), pl.ds(low, count)] = value[1]

    def pool_of(keys):
        return jnp.sum(keys.astype(F32), axis=0, keepdims=True) * (1.0 / BLOCK)

    own_block = rank * 2
    sub = BLOCK // 2
    tri_wide = lax.broadcasted_iota(jnp.int32, (sub, BLOCK), 0) <= lax.broadcasted_iota(
        jnp.int32, (sub, BLOCK), 1
    )
    tri = tri_wide[:, :sub]

    def diagonal(h, keys, block, low):
        early = tile_sum(h, keys[:sub], low, BLOCK, tri_wide)
        late = tile_sum(h, keys[sub:], low + sub, sub, tri)
        put(h, block, low, sub, tuple(None if x is None else x[:, :sub] for x in early))
        both = early[0][:, sub:] + late[0]
        top = early[1]
        if safe:
            top = jnp.maximum(early[1][:, sub:], late[1])
            both = early[0][:, sub:] * jnp.exp2((early[1][:, sub:] - top) * EXP2_SCALE) + late[
                0
            ] * jnp.exp2((late[1] - top) * EXP2_SCALE)
        put(h, block, low + sub, sub, (both, top))

    first = kbuf[rank, :BLOCK]
    second = kbuf[rank, BLOCK:]
    pool[pl.ds(own_block, 1), :] = pool_of(first)
    pool[pl.ds(own_block + 1, 1), :] = pool_of(second)
    for h in range(GROUP):
        diagonal(h, first, own_block, 0)
        put(h, own_block, BLOCK, BLOCK, tile_sum(h, first, BLOCK, BLOCK, None))
        diagonal(h, second, own_block + 1, BLOCK)

    def ship_copy(z):
        return pltpu.make_async_remote_copy(
            src_ref=ship_out.at[z],
            dst_ref=ship_in.at[z],
            send_sem=ship_send.at[z],
            recv_sem=ship_recv.at[z],
            device_id={"ctx": jnp.where(z < n_z, partner, z_mate)},
            device_id_type=MESH,
        )

    def pick(i, values):
        out = values[-1]
        for n in range(len(values) - 2, -1, -1):
            out = jnp.where(i == n, values[n], out)
        return out

    shapes = [(j, blk, part) for j in range(2) for blk in range(4) for part in range(2)]
    kept_state = (mass, peak) if safe else (mass,)
    n_steps = 9

    def lower_sib(z):
        return z * 2 + 1 - core

    def higher_sib(z):
        return half_ctx + z * 2 + 1 - core

    def step(i, _):
        low = upper == 0
        high = upper == 1

        @pl.when(low)
        def _():
            @pl.when(i == 0)
            def _():
                arrived(sibling)

            @pl.when(i == 1)
            def _():
                arrived(lower(z_next))
                backward(lower(z_next)).start()
                to_sibling(lower(z_next)).start()

            @pl.when(i == jnp.where(z_first, 6, 1))
            def _():
                arrived(lower(z_prev))
                to_sibling(lower(z_prev)).start()

            @pl.when(i == jnp.where(z_first, 7, 2))
            def _():
                arrived(lower_sib(z_prev))

            @pl.when(i == 3)
            def _():
                arrived(lower_sib(z_next))

            @pl.when(i == jnp.where(z_last, 4, 3))
            def _():
                q_ship.wait_recv()

            @pl.when(i == 4)
            def _():
                arrived(lower(z_far))
                to_sibling(lower(z_far)).start()

            @pl.when(i == 5)
            def _():
                arrived(lower_sib(z_far))

        @pl.when(high)
        def _():
            @pl.when((i == 0) & (core == 1))
            def _():
                arrived(sibling)

            @pl.when(i == 1)
            def _():
                @pl.when(zee > 0)
                def _():
                    arrived(higher(z_prev))

                    @pl.when(zee < n_z - 1)
                    def _():
                        onward(higher(z_prev)).start()

                    to_sibling(higher(z_prev)).start()

                arrived(lower(zee))
                backward(lower(zee)).start()
                onward(lower(zee)).start()
                to_sibling(lower(zee)).start()

            @pl.when((i == 2) & (zee > 0))
            def _():
                arrived(higher_sib(z_prev))

            @pl.when((i == 2) & z_last)
            def _():
                arrived(higher(0))
                to_sibling(higher(0)).start()

            @pl.when(i == 3)
            def _():
                arrived(lower_sib(zee))

                @pl.when(z_last)
                def _():
                    arrived(higher_sib(0))

            @pl.when(i == 4)
            def _():
                arrived(lower(z_next))
                backward(lower(z_next)).start()
                to_sibling(lower(z_next)).start()

                @pl.when(zee >= 2)
                def _():
                    arrived(higher(z_far))
                    to_sibling(higher(z_far)).start()

                @pl.when(z_first)
                def _():
                    arrived(higher(1))
                    to_sibling(higher(1)).start()

            @pl.when((i == 5) & (zee >= 2))
            def _():
                arrived(higher_sib(z_far))

            @pl.when(i == 6)
            def _():
                arrived(lower_sib(z_next))
                arrived(lower(z_prev))
                to_sibling(lower(z_prev)).start()

            @pl.when(i == 7)
            def _():
                arrived(lower_sib(z_prev))
                arrived(lower(z_far))
                to_sibling(lower(z_far)).start()

            @pl.when(i == 8)
            def _():
                arrived(lower_sib(z_far))

            @pl.when((i == 4) & z_first & (core == 0))
            def _():
                arrived(sibling)

            @pl.when((i == 5) & z_first)
            def _():
                arrived(higher_sib(1))

        @pl.when((i == 4) & z_first)
        def _():
            zq_ship.wait_recv()

        narrow = (i <= 2) | ((zee == n_z - 2) & ((i == 4) | (i == 5)))
        side = jnp.where((i == 1) | (i == 4), core, 1 - core)
        piece = plane + pick(i, (zee, z_prev, z_prev, 0)) * 2 + side
        z_turn = z_first & ((i == 4) | (i == 5))
        own_turn = jnp.where(low, 8, 5)
        in_plane = z_turn | (z_last & ((i == 3) | (i == own_turn)))
        here = pick(
            i,
            (
                0,
                0,
                0,
                jnp.where(z_last, 0, zee),
                jnp.where(z_first, 0, zee),
                1,
                z_next,
                z_prev,
                z_far,
            ),
        )
        first_piece = jnp.where(in_plane, plane, 0) + here * 2
        base = jnp.where(
            z_turn, GROUP + 2, jnp.where(low & jnp.logical_not(in_plane), GROUP, 0)
        )
        live = jnp.where(
            i == 0,
            core == 1,
            (zee >= pick(i, (0, 1, 1, 0, 2, 2, 0, 0, 0))) | z_turn,
        )

        @pl.when(narrow & live)
        def _():
            for half in range(2):
                keys = kbuf[piece, half * BLOCK : (half + 1) * BLOCK]
                block = piece * 2 + half
                pool[pl.ds(block, 1), :] = pool_of(keys)
                for h in range(GROUP):
                    put(h, block, 0, rows, tile_sum(h, keys, 0, rows, None))

        @pl.when(jnp.logical_not(narrow) & live)
        def _():
            for blk in range(4):
                keys = kbuf[first_piece + blk // 2, blk % 2 * BLOCK : (blk % 2 + 1) * BLOCK]
                block = first_piece * 2 + blk
                pool[pl.ds(block, 1), :] = pool_of(keys)
                for j in range(2):
                    put(base + j, block, 0, rows, tile_sum(base + j, keys, 0, rows, None))

        @pl.when(live & jnp.logical_not(narrow) & (base > 0))
        def _():
            slot = jnp.where(z_turn, n_z, 0) + here
            for k, source in enumerate(kept_state):
                for n, (j, blk, part) in enumerate(shapes):
                    ship_out[slot, k * 16 + n, :] = source[
                        base + j, first_piece * 2 + blk, part * BLOCK : (part + 1) * BLOCK
                    ]
            ship_copy(slot).start()

        return 0

    lax.fori_loop(0, n_steps, step, 0)

    def collect(low_slot, high_slot, first_block):
        def one(z, _):
            ship_copy(z).wait_recv()
            for k, target in enumerate(kept_state):
                for n, (j, blk, part) in enumerate(shapes):
                    target[
                        2 + j,
                        first_block + (z - low_slot) * 4 + blk,
                        part * BLOCK : (part + 1) * BLOCK,
                    ] = ship_in[z, k * 16 + n, :]
            return 0

        lax.fori_loop(low_slot, high_slot, one, 0)

    p1, p2, p3 = split3(pool[...])
    pool_rows = jnp.concatenate([p1, p2, p3], axis=0)
    pool_stack = jnp.concatenate([p1, p2, p3, p1, p2, p1], axis=0)
    block_id = lax.broadcasted_iota(jnp.int32, (n_block, rows), 0)
    row_block = own_block + lax.broadcasted_iota(jnp.int32, (n_block, rows), 1) // BLOCK
    allowed = block_id <= row_block
    grad_sum = jnp.zeros((n_block, D_HEAD), F32)
    entropy = jnp.zeros((1, rows), F32)
    bad = jnp.zeros((1, rows), F32)
    for h in range(GROUP):
        if h == 2:
            pl.when(z_last)(functools.partial(collect, n_z, n_z + 2, plane * 2))
            pl.when(upper == 1)(functools.partial(collect, 0, n_z, 0))
        q = q_ref[:, h * D_HEAD : (h + 1) * D_HEAD]
        g3 = lax.dot_general(pool_rows, q, NT, preferred_element_type=F32)
        logits = (g3[2 * n_block :] + g3[n_block : 2 * n_block]) + g3[:n_block]
        m = mass[h]
        if safe:
            top = jnp.max(peak[h], axis=0, keepdims=True)
            m = m * jnp.exp2((peak[h] - top) * EXP2_SCALE)
        total = jnp.sum(m, axis=0, keepdims=True)
        fine = (total > TOTAL_LOW) & (total < TOTAL_HIGH)
        bad = bad + jnp.where(fine, 0.0, 1.0)
        teacher = m / total
        top = jnp.max(jnp.where(allowed, logits, NEG_FLOOR), axis=0, keepdims=True)
        weights = jnp.where(allowed, jnp.exp(logits - top), 0.0)
        weight_sum = jnp.sum(weights, axis=0, keepdims=True)
        student = weights / weight_sum
        entropy = entropy + (
            top + jnp.log(weight_sum) - jnp.sum(teacher * logits, axis=0, keepdims=True)
        )
        e1, e2, e3 = split3(student - teacher)
        three = jnp.concatenate([e1, e2, e3], axis=0)
        parts[h] = three
        g = lax.dot_general(three, q, NN, preferred_element_type=F32)
        grad_sum = grad_sum + ((g[2 * n_block :] + g[n_block : 2 * n_block]) + g[:n_block])

    grad_sum = grad_sum * (1.0 / BLOCK)
    lane_sum = lambda x: sum(x[:, i * 128 : (i + 1) * 128] for i in range(rows // 128))
    entropy_lanes = lane_sum(entropy)
    bad_lanes = lane_sum(bad)
    for t in range(n_ctx):
        gbs[t, 0:2, :] = grad_sum[2 * t : 2 * t + 2, :]
        gbs[t, 2:3, :] = entropy_lanes
        gbs[t, 3:4, :] = bad_lanes
        gbs[t, 4:8, :] = jnp.zeros((4, 128), F32)

    def r1_copy(slot, to):
        return pltpu.make_async_remote_copy(
            src_ref=gbs.at[to],
            dst_ref=gbr.at[slot],
            send_sem=r1_send.at[to],
            recv_sem=r1_recv.at[slot],
            device_id={"ctx": to},
            device_id_type=MESH,
        )

    @pl.loop(1, n_ctx)
    def _(o):
        r1_copy(rank, lax.rem(rank + o, n_ctx)).start()

    gbr[rank] = gbs[rank]

    def grad_rows(h):
        e1 = parts[h, :n_block]
        e2 = parts[h, n_block : 2 * n_block]
        e3 = parts[h, 2 * n_block :]
        stack = jnp.concatenate([e1, e1, e1, e2, e2, e3], axis=0)
        gq_ref[:, h * D_HEAD : (h + 1) * D_HEAD] = lax.dot_general(
            stack, pool_stack, TN, preferred_element_type=F32
        )

    for h in range(GROUP):
        grad_rows(h)

    @pl.loop(1, n_ctx)
    def _(o):
        other = lax.rem(rank + o, n_ctx)
        r1_copy(other, other).wait_recv()

    whole = gbr[0]
    for t in range(1, n_ctx):
        whole = whole + gbr[t]
    gb_ref[...] = whole[0:2]
    hsend[...] = whole

    def r2_copy(slot, to):
        return pltpu.make_async_remote_copy(
            src_ref=hsend,
            dst_ref=hrecv.at[slot],
            send_sem=r2_send.at[to],
            recv_sem=r2_recv.at[slot],
            device_id={"head": to},
            device_id_type=MESH,
        )

    @pl.loop(1, n_head)
    def _(o):
        r2_copy(head, lax.rem(head + o, n_head)).start()

    hrecv[head] = whole

    @pl.loop(1, n_ctx)
    def _(o):
        r1_copy(rank, lax.rem(rank + o, n_ctx)).wait_send()

    @pl.when(upper == 0)
    def _():
        for own in (own_sibling, own_next, own_prev, own_up):
            own.wait_send()
        backward(lower(z_next)).wait_send()
        for z in (z_prev, z_next, z_far):
            to_sibling(lower(z)).wait_send()
        for z in range(n_z):
            ship_copy(z).wait_send()

    @pl.when(upper == 1)
    def _():
        q_ship.wait_send()
        backward(lower(zee)).wait_send()
        onward(lower(zee)).wait_send()
        backward(lower(z_next)).wait_send()
        for z in range(n_z):
            to_sibling(lower(z)).wait_send()

        @pl.when((core == 0) | z_first)
        def _():
            own_sibling.wait_send()

        @pl.when(zee < n_z - 1)
        def _():
            own_next.wait_send()

        @pl.when(zee <= 1)
        def _():
            own_prev.wait_send()

        @pl.when(z_first)
        def _():
            to_sibling(higher(1)).wait_send()

        @pl.when((zee > 0) & (zee < n_z - 1))
        def _():
            onward(higher(z_prev)).wait_send()

        @pl.loop(0, zee)
        def _(z):
            to_sibling(higher(z)).wait_send()

    @pl.when(z_last)
    def _():
        zq_ship.wait_send()

    @pl.when(z_first)
    def _():
        for z in range(n_z, n_z + 2):
            ship_copy(z).wait_send()

    @pl.loop(1, n_head)
    def _(o):
        other = lax.rem(head + o, n_head)
        r2_copy(other, other).wait_recv()

    final = hrecv[0]
    for t in range(1, n_head):
        final = final + hrecv[t]
    sums = jnp.sum(final, axis=1, keepdims=True)
    loss_ref[...] = sums[2:3] * (1.0 / (rows * n_ctx * HEADS))
    bad_ref[...] = sums[3:4]

    @pl.loop(1, n_head)
    def _(o):
        other = lax.rem(head + o, n_head)
        r2_copy(head, other).wait_send()


def run(safe, n_ctx, n_head, queries, keys):
    rows = queries.shape[0]
    n_block = n_ctx * rows // BLOCK
    half_ctx = n_ctx // 2
    ship_rows = 32 if safe else 16
    dma = pltpu.SemaphoreType.DMA
    return pl.pallas_call(
        functools.partial(kernel, safe, n_ctx, n_head),
        out_shape=(
            jax.ShapeDtypeStruct((rows, GROUP * D_HEAD), F32),
            jax.ShapeDtypeStruct((rows // BLOCK, D_HEAD), F32),
            jax.ShapeDtypeStruct((1, 1), F32),
            jax.ShapeDtypeStruct((1, 1), F32),
        ),
        in_specs=[pl.BlockSpec(memory_space=pl.ANY)] * 2,
        out_specs=(pl.BlockSpec(memory_space=pltpu.VMEM),) * 4,
        scratch_shapes=[
            pltpu.VMEM((rows, (GROUP + 4) * D_HEAD), BF16),
            pltpu.VMEM((n_ctx, rows, D_HEAD), BF16),
            pltpu.VMEM((GROUP + 4, n_block, rows), F32),
            pltpu.VMEM((GROUP + 4, n_block, rows) if safe else (8, 128), F32),
            pltpu.VMEM((n_block, D_HEAD), F32),
            pltpu.VMEM((GROUP, 3 * n_block, rows), BF16),
            pltpu.VMEM((half_ctx // 2 + 2, ship_rows, BLOCK), F32),
            pltpu.VMEM((half_ctx // 2 + 2, ship_rows, BLOCK), F32),
            pltpu.VMEM((n_ctx, 8, 128), F32),
            pltpu.VMEM((n_ctx, 8, 128), F32),
            pltpu.VMEM((8, 128), F32),
            pltpu.VMEM((n_head, 8, 128), F32),
            dma((2,)),
            dma((2,)),
            dma((4,)),
            dma((n_ctx,)),
            dma((n_ctx,)),
            dma((n_ctx,)),
            dma((n_ctx,)),
            dma((half_ctx,)),
            dma((half_ctx,)),
            dma((2,)),
            dma((n_ctx,)),
            dma((n_ctx,)),
            dma((n_head,)),
            dma((n_head,)),
        ],
        compiler_params=pltpu.CompilerParams(
            collective_id=1 if safe else 0,
            has_side_effects=True,
            vmem_limit_bytes=48 * 1024 * 1024,
        ),
        name="gate_safe" if safe else "gate_fast",
    )(queries, keys)


def solution(mesh):
    n_ctx, n_head = mesh.shape["ctx"], mesh.shape["head"]

    def local(queries, keys):
        fast = run(False, n_ctx, n_head, queries, keys)
        ok = fast[3].reshape(()) == 0.0
        out = lax.cond(
            ok,
            lambda: fast[:3],
            lambda: run(True, n_ctx, n_head, queries, keys)[:3],
        )
        return out[0], out[1], out[2].reshape(())

    return jax.shard_map(
        local,
        mesh=mesh,
        in_specs=(P("ctx", "head"), P("ctx", "head")),
        out_specs=(P("ctx", "head"), P("ctx", "head"), P()),
        check_vma=False,
    )
```
